32 devices in a mesh: ctx: 16 (over z, y, core), shard: 2 (over x).
Axes of the slice: x: 2, y: 2, z: 4, core: 2. Of those that a mesh axis runs over, the one named last changes fastest.
Arguments:
- tokens: bfloat16 [2, 8192, 1024], P('shard', 'ctx'), may hold values from -6 to 6
- teacher: bfloat16 [2, 8192, 1024], P('shard', 'ctx'), may hold values from -6 to 6
- cotangent: bfloat16 [2, 8192, 1024], P('shard', 'ctx'), may hold values from -6 to 6
- doc_starts: int32 [2, 18], P('shard'), may hold values from 0 to 8192, as said below
- doc_time: int32 [2, 18], P('shard'), may hold values from 0 to 999
- valid_mask: int32 [2, 8192], P('shard', 'ctx'), may hold values from 0 to 1, as said below
- gain_one: bfloat16 [1024], P('shard'), may hold values from 0.5 to 1.5
- bias_one: bfloat16 [1024], P('shard'), may hold values from -4 to 4
- time_one: bfloat16 [256, 1024], P('shard'), may hold values from -0.375 to 0.375
- qkv_weight: bfloat16 [1024, 3072], P('shard'), may hold values from -0.1875 to 0.1875
- out_weight: bfloat16 [1024, 1024], P('shard'), may hold values from -1.5 to 1.5
- gain_two: bfloat16 [1024], P('shard'), may hold values from 0.5 to 1.5
- bias_two: bfloat16 [1024], P('shard'), may hold values from -4 to 4
- time_two: bfloat16 [256, 1024], P('shard'), may hold values from -0.375 to 0.375
- up_weight: bfloat16 [1024, 4096], P('shard'), may hold values from -0.1875 to 0.1875
- up_bias: bfloat16 [4096], P('shard'), may hold values from -4 to 4
- down_weight: bfloat16 [4096, 1024], P('shard'), may hold values from -0.09375 to 0.09375
- down_bias: bfloat16 [1024], P('shard'), may hold values from -4 to 4
Outputs:
- output: bfloat16 [2, 8192, 1024], P('shard', 'ctx')
- loss_value: float32 [], replicated
- input_grad: float32 [2, 8192, 1024], P('shard', 'ctx')
- grad_gain_one: float32 [1024], P('shard')
- grad_bias_one: float32 [1024], P('shard')
- grad_time_one: float32 [256, 1024], P('shard')
- grad_qkv_weight: float32 [1024, 3072], P('shard')
- grad_out_weight: float32 [1024, 1024], P('shard')
- grad_gain_two: float32 [1024], P('shard')
- grad_bias_two: float32 [1024], P('shard')
- grad_time_two: float32 [256, 1024], P('shard')
- grad_up_weight: float32 [1024, 4096], P('shard')
- grad_up_bias: float32 [4096], P('shard')
- grad_down_weight: float32 [4096, 1024], P('shard')
- grad_down_bias: float32 [1024], P('shard')
The draws below stay inside these ranges and needn't reach their ends.
Inputs may be any that keep to these rules, and one draw needn't show every extreme that they name: `doc_starts`: each pack's row begins with 0 and never falls; every entry below 8192 opens a document that runs to the next larger entry (or to 8192) and has 1 to 2048 tokens; every pack has a document of exactly 2048 tokens; slots past the pack's end, the last slot among them, hold 8192. `valid_mask`: the last token of every pack has 1.
All inputs are finite; a program needn't handle non-finite values.
Results may differ from the reference program's by a relative error of at most 0.024.
Values may be sent and summed in bfloat16 or wider, within the bound.
No kernel may reach another device: no remote copies, remote signals or barrier semaphores. Data moves between devices by JAX's collectives and lax.ppermute only.
A program may use at most 320 MiB of HBM per device.

```python
import math
import jax
import jax.numpy as jnp
from jax import lax

D = 1024
HEADS = 16
HEAD = 64
FF = 4096
TEMB = 256
TSTEPS = 1000
SEQ = 8192
PACKS = 2
DOC_MAX = 2048
DOC_SLOTS = 18


def draw_doc_starts(key, part):

    def per_pack(pack_key):
        first_key = jax.random.fold_in(pack_key, 1)
        pick_key = jax.random.fold_in(pack_key, 2)
        lengths_all = jax.random.randint(first_key, (DOC_SLOTS,), DOC_MAX // 4, DOC_MAX + 1)
        chosen = jax.random.randint(pick_key, (), 0, 2)
        lengths_all = jnp.where(jnp.arange(DOC_SLOTS) == chosen, DOC_MAX, lengths_all)
        finish = jnp.cumsum(lengths_all)
        return jnp.minimum(finish - lengths_all, SEQ).astype(jnp.int32)
    pack_keys = jax.random.split(jax.random.fold_in(key, 7), PACKS)
    return jax.vmap(per_pack)(pack_keys)


def draw_valid_mask(key, part):
    places = jnp.arange(SEQ, dtype=jnp.int32)
    tickets = jax.random.randint(jax.random.fold_in(key, 11), (PACKS, SEQ), 0, 4 * SEQ)
    chosen = jnp.logical_or(tickets < SEQ + 2 * places[None, :], places[None, :] == SEQ - 1)
    return chosen.astype(jnp.int32)


def with_ends(array, own_key, low, largest):
    spot = [jax.random.randint(jax.random.fold_in(own_key, axis), (), 0, length) for axis, length in enumerate(array.shape)]
    widest = array.shape.index(max(array.shape))
    beside = spot[:widest] + [(spot[widest] + 1) % array.shape[widest]] + spot[widest + 1:]
    return array.at[tuple(spot)].set(low).at[tuple(beside)].set(largest)


def block_levels(key, shape, shards, low, largest):
    gain = 1.0
    for dim, shards_of in shards:
        draws = jax.random.uniform(jax.random.fold_in(jax.random.fold_in(key, 6), dim), (shards_of,), jnp.float32, low / len(shards), largest / len(shards))
        gain = gain * jnp.repeat(jnp.exp(draws), shape[dim] // shards_of).reshape((-1,) + (1,) * (len(shape) - 1 - dim))
    return gain


def gaussian(rng, extent, width, reach, cuts=(), kind=jnp.bfloat16):
    entries = jax.random.normal(rng, extent, jnp.float32) * width
    if len(cuts) > 0:
        entries = block_levels(rng, extent, cuts, -0.22, 0.18) * entries
    return jnp.clip(entries, min=-reach, max=reach).astype(kind)


def setup_inputs(seed: int = 0) -> dict:
    arg_keys = jax.random.split(jax.random.key(seed), 19)
    return {
        "tokens": gaussian(arg_keys[0], (PACKS, SEQ, D), 1.0, 6.0, ((0, 2), (1, 16))),
        "teacher": gaussian(arg_keys[1], (PACKS, SEQ, D), 1.0, 6.0, ((0, 2), (1, 16))),
        "cotangent": gaussian(arg_keys[2], (PACKS, SEQ, D), 1.0, 6.0, ((0, 2), (1, 16))),
        "doc_starts": draw_doc_starts(jax.random.fold_in(arg_keys[18], 71), 0),
        "doc_time": with_ends(jax.random.randint(arg_keys[4], (PACKS, DOC_SLOTS), 0, TSTEPS), jax.random.fold_in(arg_keys[4], 1), 0, TSTEPS - 1).astype(jnp.int32),
        "valid_mask": draw_valid_mask(jax.random.fold_in(arg_keys[18], 71), 0),
        "gain_one": jnp.clip(1.0 + 0.1 * jax.random.normal(arg_keys[6], (D,), jnp.float32), 0.5, 1.5).astype(jnp.bfloat16),
        "bias_one": gaussian(arg_keys[7], (D,), 0.3, 4.0, ((0, 2),)),
        "time_one": gaussian(arg_keys[8], (TEMB, D), TEMB ** -0.5, 0.375, ((0, 2),)),
        "qkv_weight": gaussian(arg_keys[9], (D, 3 * D), D ** -0.5, 0.1875, ((0, 2),)),
        "out_weight": gaussian(arg_keys[10], (D, D), (D // 64) ** -0.5, 1.5, ((0, 2),)),
        "gain_two": jnp.clip(1.0 + 0.1 * jax.random.normal(arg_keys[11], (D,), jnp.float32), 0.5, 1.5).astype(jnp.bfloat16),
        "bias_two": gaussian(arg_keys[12], (D,), 0.3, 4.0, ((0, 2),)),
        "time_two": gaussian(arg_keys[13], (TEMB, D), TEMB ** -0.5, 0.375, ((0, 2),)),
        "up_weight": gaussian(arg_keys[14], (D, FF), D ** -0.5, 0.1875, ((0, 2),)),
        "up_bias": gaussian(arg_keys[15], (FF,), 0.3, 4.0, ((0, 2),)),
        "down_weight": gaussian(arg_keys[16], (FF, D), FF ** -0.5, 0.09375, ((0, 2),)),
        "down_bias": gaussian(arg_keys[17], (D,), 0.3, 4.0, ((0, 2),)),
    }


@jax.custom_vjp
def low(v):
    return lax.optimization_barrier(v.astype(jnp.bfloat16)).astype(jnp.float32)

@jax.custom_vjp
def low_back(v):
    return v

def low_keep(v):
    return (low(v), None)

def low_pass(kept, grad):
    return (grad,)

def back_keep(v):
    return (v, None)

def back_low(kept, grad):
    return (low(grad),)
low.defvjp(low_keep, low_pass)
low_back.defvjp(back_keep, back_low)
norm_eps = 1e-05
masked_value = -1e+30

def doc_fields(starts, stamps, places):
    inside = starts[None, :] <= places[:, None]
    segment = lax.optimization_barrier(jnp.sum(inside.astype(jnp.int32), axis=1)) - 1
    doc_begin = lax.optimization_barrier(jnp.max(jnp.where(inside, starts[None, :], 0), axis=1))
    slot_ids = jnp.arange(starts.shape[0], dtype=jnp.int32)
    time_index = lax.optimization_barrier(jnp.sum(jnp.where(segment[:, None] == slot_ids[None, :], stamps[None, :], 0), axis=1))
    return (segment, places - doc_begin, time_index)

def time_features(time_index):
    halfway = TEMB // 2
    ladder = jnp.exp(-math.log(10000.0) * jnp.arange(halfway, dtype=jnp.float32) / halfway)
    phases = time_index.astype(jnp.float32)[:, None] * ladder[None, :]
    return jnp.concatenate([jnp.sin(phases), jnp.cos(phases)], axis=1)

def rotate(vectors, places):
    count_rows = vectors.shape[0]
    halfway = HEAD // 2
    ladder = jnp.exp(-math.log(10000.0) * 2.0 * jnp.arange(halfway, dtype=jnp.float32) / HEAD)
    turned = places.astype(jnp.float32)[:, None] * ladder[None, :]
    cosine = jnp.cos(turned)[:, None, :]
    sine_part = jnp.sin(turned)[:, None, :]
    split_heads = vectors.reshape(count_rows, HEADS, HEAD)
    former = split_heads[:, :, :halfway]
    latter = split_heads[:, :, halfway:]
    joined = jnp.concatenate([former * cosine - latter * sine_part, former * sine_part + latter * cosine], axis=2)
    return joined.reshape(count_rows, HEADS * HEAD)

def scaled_norm(values, gain_vec, bias_vec, feats_low, time_weight):
    average = lax.optimization_barrier(jnp.mean(values, axis=1, keepdims=True))
    centred = values - average
    normed = centred * lax.rsqrt(lax.optimization_barrier(jnp.mean(centred * centred, axis=1, keepdims=True)) + norm_eps)
    scales = gain_vec[None, :] + low_back(jnp.dot(feats_low, time_weight, precision=lax.Precision.HIGHEST))
    return normed * scales + bias_vec[None, :]

def attend(query_all, key_all, value_all, segment):
    length = query_all.shape[0]
    query_block = math.gcd(length, 512)
    key_heads = key_all.reshape(length, HEADS, HEAD)
    value_heads = value_all.reshape(length, HEADS, HEAD)

    def per_block(block_num):
        first_row = block_num * query_block
        query_heads = lax.dynamic_slice_in_dim(query_all, first_row, query_block, 0).reshape(query_block, HEADS, HEAD)
        query_seg = lax.dynamic_slice_in_dim(segment, first_row, query_block, 0)
        raw_scores = low_back(jnp.einsum('qhd,khd->hqk', query_heads, key_heads, precision=lax.Precision.HIGHEST)) * HEAD ** (-0.5)
        scores = jnp.where((query_seg[:, None] == segment[None, :])[None], raw_scores, masked_value)
        top_score = lax.optimization_barrier(jnp.max(scores, axis=2, keepdims=True))
        log_total = top_score + jnp.log(lax.optimization_barrier(jnp.sum(jnp.exp(scores - top_score), axis=2, keepdims=True)))
        prob_low = low(jnp.exp(scores - log_total))
        mixed_part = jnp.einsum('hqk,khd->qhd', prob_low, value_heads, precision=lax.Precision.HIGHEST)
        return mixed_part.reshape(query_block, HEADS * HEAD)
    pieces = lax.map(jax.checkpoint(per_block), jnp.arange(length // query_block, dtype=jnp.int32))
    return pieces.reshape(length, HEADS * HEAD)

def pack_layer(block_in, features, segment, places, params):
    gain_one, bias_one, time_one, qkv_weight, out_weight, gain_two, bias_two, time_two, up_weight, up_bias, down_weight, down_bias = params
    feats_low = low(features)
    act_one = low(scaled_norm(block_in, gain_one, bias_one, feats_low, time_one))
    joined = low_back(jnp.dot(act_one, qkv_weight, precision=lax.Precision.HIGHEST))
    query_all = low(rotate(joined[:, :D], places))
    key_all = low(rotate(joined[:, D:2 * D], places))
    value_all = low(joined[:, 2 * D:])
    mixed_out = low(low_back(attend(query_all, key_all, value_all, segment)))
    middle = block_in + low_back(jnp.dot(mixed_out, out_weight, precision=lax.Precision.HIGHEST))
    act_two = low(scaled_norm(middle, gain_two, bias_two, feats_low, time_two))
    upper_in = low_back(jnp.dot(act_two, up_weight, precision=lax.Precision.HIGHEST) + up_bias[None, :])
    hidden = low(jax.nn.gelu(upper_in, approximate=False))
    return middle + low_back(jnp.dot(hidden, down_weight, precision=lax.Precision.HIGHEST) + down_bias[None, :])

def reference(tokens, teacher, cotangent, doc_starts, doc_time, valid_mask, gain_one, bias_one, time_one, qkv_weight, out_weight, gain_two, bias_two, time_two, up_weight, up_bias, down_weight, down_bias):
    all_places = jnp.arange(SEQ, dtype=jnp.int32)
    segment, places_all, time_all = jax.vmap(lambda starts_row, times_row: doc_fields(starts_row, times_row, all_places))(doc_starts, doc_time)
    features = jax.vmap(time_features)(time_all)
    params = tuple((weight_arg.astype(jnp.float32) for weight_arg in (gain_one, bias_one, time_one, qkv_weight, out_weight, gain_two, bias_two, time_two, up_weight, up_bias, down_weight, down_bias)))
    weight_mask = valid_mask.astype(jnp.float32)
    target = teacher.astype(jnp.float32)

    def objective(block_in, params_in):

        def per_pack(pack_item):
            pack_in, pack_feats, pack_seg, pack_places = pack_item
            return pack_layer(pack_in, pack_feats, pack_seg, pack_places, params_in)
        block_out = lax.map(per_pack, (block_in, features, segment, places_all))
        counted = jnp.sum(weight_mask)
        misfit = block_out - target
        loss_value = jnp.sum(weight_mask[:, :, None] * misfit * misfit) / (counted * D)
        return (block_out, loss_value)
    (block_out, loss_value), pull_back = jax.vjp(objective, tokens.astype(jnp.float32), params)
    input_grad, weight_grads = pull_back((cotangent.astype(jnp.float32), jnp.ones((), jnp.float32)))
    return (block_out.astype(jnp.bfloat16), loss_value, input_grad, weight_grads[0], weight_grads[1], weight_grads[2], weight_grads[3], weight_grads[4], weight_grads[5], weight_grads[6], weight_grads[7], weight_grads[8], weight_grads[9], weight_grads[10], weight_grads[11])
```

```python
import math

import jax
import jax.numpy as jnp
from jax import lax
from jax.experimental import pallas as pl
from jax.experimental.pallas import tpu as pltpu
from jax.sharding import Mesh
from jax.sharding import PartitionSpec as P

HEADS = 16
HEAD = 64
TEMB = 256
QUAD = 4
LOCAL_HEADS = HEADS // QUAD
LANES = 128
BLOCK_Q = 256
BLOCK_K = 256
norm_eps = 1e-05
masked_value = -1e30
LOG2E = math.log2(math.e)
bf16 = jnp.bfloat16
f32 = jnp.float32


def flip(value, axis):
    return lax.ppermute(value, axis, [(0, 1), (1, 0)])


def in_order(index, own, other, axis):
    return jnp.where(
        index == 0,
        jnp.concatenate([own, other], axis=axis),
        jnp.concatenate([other, own], axis=axis),
    )


def half_of(value, index):
    rows = value.shape[0] // 2
    return lax.dynamic_slice_in_dim(value, index * rows, rows, 0)


def xor_pairs(size, bit):
    return [(i, i ^ bit) for i in range(size)]


def bits_of(axis):
    return [1 << b for b in range(lax.axis_size(axis).bit_length() - 1)]


def scatter_sum(value, axis):
    size = lax.axis_size(axis)
    for bit in bits_of(axis):
        mine = (lax.axis_index(axis) // bit) % 2
        sent = half_of(value, 1 - mine).astype(bf16)
        got = lax.ppermute(sent, axis, xor_pairs(size, bit))
        value = half_of(value, mine).astype(f32) + got.astype(f32)
    return value


def gather_back(value, axis):
    size = lax.axis_size(axis)
    for bit in reversed(bits_of(axis)):
        mine = (lax.axis_index(axis) // bit) % 2
        got = lax.ppermute(value, axis, xor_pairs(size, bit))
        value = in_order(mine, value, got, 0)
    return value


def sum_all(value, axis):
    size = lax.axis_size(axis)
    for bit in bits_of(axis):
        value = value + lax.ppermute(value, axis, xor_pairs(size, bit))
    return value


def gather_shard(value):
    if lax.axis_size("shard") == 2:
        return in_order(lax.axis_index("shard"), value, flip(value, "shard"), 0)
    return lax.all_gather(value, "shard", axis=0, tiled=True)


def contract_rows(left_side, right_side):
    return lax.dot_general(
        left_side, right_side, (((0,), (0,)), ((), ())), preferred_element_type=f32
    )


def times_trans(left_side, right_side):
    return lax.dot_general(
        left_side, right_side, (((1,), (1,)), ((), ())), preferred_element_type=f32
    )


def times(left_side, right_side):
    return jnp.dot(left_side, right_side, preferred_element_type=f32)


def segments_at(starts, places):
    return jnp.sum((starts[None, :] <= places[:, None]).astype(jnp.int32), axis=1) - 1


def begins_at(starts, places):
    return jnp.max(jnp.where(starts[None, :] <= places[:, None], starts[None, :], 0), axis=1)


def ends_at(starts, places, length):
    return jnp.min(jnp.where(starts[None, :] > places[:, None], starts[None, :], length), axis=1)


def block_ranges(starts, length, row_base, row_block, col_base, col_block, tokens):
    count = tokens // row_block
    first = row_base + row_block * jnp.arange(count, dtype=jnp.int32)
    last = first + row_block - 1
    real = jnp.logical_and(first >= 0, last < length)
    begin_first = begins_at(starts, first)
    low = jnp.clip(begin_first - col_base, 0, tokens)
    high = jnp.clip(ends_at(starts, last, length) - col_base, 0, tokens)
    live = jnp.logical_and(real, high > low)
    low_block = jnp.where(live, low // col_block, 0)
    high_block = jnp.where(live, (high + col_block - 1) // col_block, 0)
    whole = jnp.logical_and(live, begin_first == begins_at(starts, last))
    full_low = jnp.where(whole, (low + col_block - 1) // col_block, high_block)
    full_high = jnp.where(whole, high // col_block, high_block)
    full_low = jnp.minimum(full_low, high_block)
    full_high = jnp.clip(full_high, full_low, high_block)
    return jnp.stack([low_block, full_low, full_high, high_block]).astype(jnp.int32)


def time_features(time_index):
    halfway = TEMB // 2
    ladder = jnp.exp(-math.log(10000.0) * jnp.arange(halfway, dtype=f32) / halfway)
    phases = time_index.astype(f32)[:, None] * ladder[None, :]
    return jnp.concatenate([jnp.sin(phases), jnp.cos(phases)], axis=1)


def turn_tables(places):
    halfway = HEAD // 2
    ladder = jnp.exp(-math.log(10000.0) * 2.0 * jnp.arange(halfway, dtype=f32) / HEAD)
    wide = jnp.tile(ladder, LOCAL_HEADS * 2)
    turned = places.astype(f32)[:, None] * wide[None, :]
    lane = jnp.arange(LOCAL_HEADS * HEAD) % HEAD
    sign = jnp.where(lane < halfway, -1.0, 1.0).astype(f32)
    return jnp.cos(turned), jnp.sin(turned) * sign[None, :]


def turn(vectors, cosine, signed_sine):
    halfway = HEAD // 2
    lane = jnp.arange(LOCAL_HEADS * HEAD) % HEAD
    from_right = jnp.concatenate([vectors[:, halfway:], vectors[:, :halfway]], axis=1)
    from_left = jnp.concatenate([vectors[:, -halfway:], vectors[:, :-halfway]], axis=1)
    partner = jnp.where((lane < halfway)[None, :], from_right, from_left)
    return vectors * cosine + partner * signed_sine


def norm_forward(values, gain_vec, bias_vec, features, time_weight):
    average = jnp.mean(values, axis=1, keepdims=True)
    centred = values - average
    inv_std = lax.rsqrt(jnp.mean(centred * centred, axis=1, keepdims=True) + norm_eps)
    normed = centred * inv_std
    scales = gain_vec.astype(f32)[None, :] + times(features, time_weight)
    return (normed * scales + bias_vec.astype(f32)[None, :], normed, scales, inv_std)


def norm_backward(grad_act, normed, scales, inv_std, one_hot):
    grad_scale = grad_act * normed
    grad_gain = jnp.sum(grad_scale, axis=0, keepdims=True)
    grad_bias = jnp.sum(grad_act, axis=0, keepdims=True)
    by_doc = contract_rows(one_hot, grad_scale.astype(bf16))
    grad_norm = grad_act * scales
    grad_input = inv_std * (
        grad_norm
        - jnp.mean(grad_norm, axis=1, keepdims=True)
        - normed * jnp.mean(grad_norm * normed, axis=1, keepdims=True)
    )
    return (grad_input, grad_gain, grad_bias, by_doc)


def lane_halves(value):
    lane = lax.broadcasted_iota(jnp.int32, value.shape, 1)
    zero = jnp.zeros_like(value)
    return jnp.where(lane < HEAD, value, zero), jnp.where(lane < HEAD, zero, value)


def dot_last(left_side, right_side):
    return lax.dot_general(
        left_side, right_side, (((1,), (1,)), ((), ())), preferred_element_type=f32
    )


def look_through(bounds, step, query_pair, kv_ref, pair, seg_q, seg_row, state):
    left, right = lane_halves(query_pair)
    lane = lax.broadcasted_iota(jnp.int32, (BLOCK_Q, LANES), 1)
    key_lanes = slice(pair * LANES, (pair + 1) * LANES)
    value_base = LOCAL_HEADS * HEAD + pair * LANES
    value_lanes = slice(value_base, value_base + LANES)

    def visit(masked):
        def body(block, carried):
            tops, totals, acc = carried
            rows = pl.ds(pl.multiple_of(block * BLOCK_K, BLOCK_K), BLOCK_K)
            keys = kv_ref[rows, key_lanes]
            values = lane_halves(kv_ref[rows, value_lanes])
            if masked:
                allowed = seg_q == seg_row(block)
            new_tops, new_totals, scales, extra = [], [], [], None
            for side, query in enumerate((left, right)):
                scores = dot_last(query, keys)
                if masked:
                    scores = jnp.where(allowed, scores, masked_value)
                top = jnp.maximum(tops[side], jnp.max(scores, axis=1, keepdims=True))
                weights = jnp.exp2(scores - top)
                scale = jnp.exp2(tops[side] - top)
                new_tops.append(top)
                new_totals.append(
                    totals[side] * scale + jnp.sum(weights, axis=1, keepdims=True)
                )
                scales.append(scale)
                part = times(weights.astype(bf16), values[side])
                extra = part if extra is None else extra + part
            acc = acc * jnp.where(lane < HEAD, scales[0], scales[1]) + extra
            return tuple(new_tops), tuple(new_totals), acc

        return body

    low, full_low, full_high, high = (bounds[k, step] for k in range(4))
    state = lax.fori_loop(low, full_low, visit(True), state)
    state = lax.fori_loop(full_low, full_high, visit(False), state)
    return lax.fori_loop(full_high, high, visit(True), state)


def pick_lane(tile, lane):
    return tile[:, lane : lane + 1]


def near_kernel(bounds, query_ref, kv_ref, seg_q_ref, seg_k_ref, acc_ref, stat_ref):
    step = pl.program_id(0)
    seg_q = seg_q_ref[...]

    def seg_row(block):
        return seg_k_ref[1:2, pl.ds(pl.multiple_of(block * BLOCK_K, BLOCK_K), BLOCK_K)]

    lane = lax.broadcasted_iota(jnp.int32, (BLOCK_Q, LANES), 1)
    stat = jnp.zeros((BLOCK_Q, LANES), f32)
    for pair in range(LOCAL_HEADS // 2):
        top = jnp.full((BLOCK_Q, 1), masked_value, f32)
        total = jnp.zeros((BLOCK_Q, 1), f32)
        acc = jnp.zeros((BLOCK_Q, LANES), f32)
        query_pair = query_ref[:, pair * LANES : (pair + 1) * LANES]
        tops, totals, acc = look_through(
            bounds, step, query_pair, kv_ref, pair, seg_q, seg_row, ((top, top), (total, total), acc)
        )
        acc_ref[:, pair * LANES : (pair + 1) * LANES] = acc
        for side in range(2):
            head = 2 * pair + side
            stat = jnp.where(lane == head, tops[side], stat)
            stat = jnp.where(lane == LOCAL_HEADS + head, totals[side], stat)
    stat_ref[...] = stat


def far_kernel(
    before, after, query_ref, prev_ref, next_ref, seg_q_ref, seg_k_ref, acc_in, stat_in, out_ref, lse_ref
):
    step = pl.program_id(0)
    seg_q = seg_q_ref[...]
    lane = lax.broadcasted_iota(jnp.int32, (BLOCK_Q, LANES), 1)
    stat = stat_in[...]
    lse_tile = jnp.zeros((BLOCK_Q, LANES), f32)
    for pair in range(LOCAL_HEADS // 2):
        lanes = slice(pair * LANES, (pair + 1) * LANES)
        tops = tuple(pick_lane(stat, 2 * pair + side) for side in range(2))
        totals = tuple(pick_lane(stat, LOCAL_HEADS + 2 * pair + side) for side in range(2))
        state = (tops, totals, acc_in[:, lanes])
        for row, bounds, kv_ref in ((0, before, prev_ref), (2, after, next_ref)):

            def seg_row(block, row=row):
                columns = pl.ds(pl.multiple_of(block * BLOCK_K, BLOCK_K), BLOCK_K)
                return seg_k_ref[row : row + 1, columns]

            state = look_through(
                bounds, step, query_ref[:, lanes], kv_ref, pair, seg_q, seg_row, state
            )
        tops, totals, acc = state
        share = jnp.where(lane < HEAD, totals[0], totals[1])
        out_ref[:, lanes] = (acc / share).astype(out_ref.dtype)
        for side in range(2):
            lse = tops[side] + jnp.log2(totals[side])
            lse_tile = jnp.where(lane == 2 * pair + side, lse, lse_tile)
    lse_ref[...] = jnp.transpose(lse_tile)[:8, :]


def attend_near(bounds, query, kv_pair, seg_q, seg_k):
    tokens, width = query.shape
    return pl.pallas_call(
        near_kernel,
        out_shape=(
            jax.ShapeDtypeStruct((tokens, width), f32),
            jax.ShapeDtypeStruct((tokens, LANES), f32),
        ),
        grid_spec=pltpu.PrefetchScalarGridSpec(
            num_scalar_prefetch=1,
            grid=(tokens // BLOCK_Q,),
            in_specs=[
                pl.BlockSpec((BLOCK_Q, width), lambda i, b: (i, 0)),
                pl.BlockSpec((tokens, 2 * width), lambda i, b: (0, 0)),
                pl.BlockSpec((BLOCK_Q, 1), lambda i, b: (i, 0)),
                pl.BlockSpec((8, tokens), lambda i, b: (0, 0)),
            ],
            out_specs=(
                pl.BlockSpec((BLOCK_Q, width), lambda i, b: (i, 0)),
                pl.BlockSpec((BLOCK_Q, LANES), lambda i, b: (i, 0)),
            ),
        ),
        name="attend_near",
    )(bounds, query, kv_pair, seg_q, seg_k)


def attend_far(before, after, query, kv_prev, kv_next, seg_q, seg_k, acc, stat):
    tokens, width = query.shape
    return pl.pallas_call(
        far_kernel,
        out_shape=(
            jax.ShapeDtypeStruct((tokens, width), bf16),
            jax.ShapeDtypeStruct((8, tokens), f32),
        ),
        grid_spec=pltpu.PrefetchScalarGridSpec(
            num_scalar_prefetch=2,
            grid=(tokens // BLOCK_Q,),
            in_specs=[
                pl.BlockSpec((BLOCK_Q, width), lambda i, b, a: (i, 0)),
                pl.BlockSpec((tokens, 2 * width), lambda i, b, a: (0, 0)),
                pl.BlockSpec((tokens, 2 * width), lambda i, b, a: (0, 0)),
                pl.BlockSpec((BLOCK_Q, 1), lambda i, b, a: (i, 0)),
                pl.BlockSpec((8, tokens), lambda i, b, a: (0, 0)),
                pl.BlockSpec((BLOCK_Q, width), lambda i, b, a: (i, 0)),
                pl.BlockSpec((BLOCK_Q, LANES), lambda i, b, a: (i, 0)),
            ],
            out_specs=(
                pl.BlockSpec((BLOCK_Q, width), lambda i, b, a: (i, 0)),
                pl.BlockSpec((8, BLOCK_Q), lambda i, b, a: (0, i)),
            ),
        ),
        name="attend_far",
    )(before, after, query, kv_prev, kv_next, seg_q, seg_k, acc, stat)


def return_kernel(
    bounds, query_ref, grad_ref, kv_ref, seg_k_ref, seg_q_ref, lse_ref, delta_ref, dq_in, dq_ref, dkv_ref
):
    step = pl.program_id(0)
    width = LOCAL_HEADS * HEAD

    @pl.when(step == 0)
    def _():
        dq_ref[...] = dq_in[...]

    seg_k = seg_k_ref[...]
    low, full_low, full_high, high = (bounds[k, step] for k in range(4))
    for pair in range(LOCAL_HEADS // 2):
        lanes = slice(pair * LANES, (pair + 1) * LANES)
        keys = lane_halves(kv_ref[:, lanes])
        values = lane_halves(kv_ref[:, width + pair * LANES : width + (pair + 1) * LANES])

        def visit(masked, pair=pair, lanes=lanes, keys=keys, values=values):
            def body(block, carried):
                dk, dv = carried
                rows = pl.ds(pl.multiple_of(block * BLOCK_Q, BLOCK_Q), BLOCK_Q)
                query_pair = query_ref[rows, lanes]
                grad_pair = grad_ref[rows, lanes]
                queries = lane_halves(query_pair)
                grads = lane_halves(grad_pair)
                if masked:
                    allowed = seg_k == seg_q_ref[0:1, rows]
                dq = None
                for side in range(2):
                    head = 2 * pair + side
                    scores = dot_last(keys[side], query_pair) - lse_ref[head : head + 1, rows]
                    if masked:
                        scores = jnp.where(allowed, scores, masked_value)
                    prob = jnp.exp2(scores)
                    grad_prob = dot_last(values[side], grad_pair) - delta_ref[head : head + 1, rows]
                    grad_scores = (prob * grad_prob).astype(bf16)
                    dv = dv + times(prob.astype(bf16), grads[side])
                    dk = dk + times(grad_scores, queries[side])
                    part = contract_rows(grad_scores, keys[side])
                    dq = part if dq is None else dq + part
                dq_ref[rows, lanes] += dq
                return dk, dv

            return body

        start = jnp.zeros((BLOCK_K, LANES), f32)
        state = lax.fori_loop(low, full_low, visit(True), (start, start))
        state = lax.fori_loop(full_low, full_high, visit(False), state)
        dk, dv = lax.fori_loop(full_high, high, visit(True), state)
        dkv_ref[:, lanes] = (dk * (1.0 / LOG2E)).astype(dkv_ref.dtype)
        dkv_ref[:, width + pair * LANES : width + (pair + 1) * LANES] = dv.astype(dkv_ref.dtype)


def attend_return(bounds, query, grad, kv_pair, seg_k, seg_q, lse, delta, dq):
    tokens, width = query.shape

    def whole(shape):
        return pl.BlockSpec(shape, lambda i, b: (0, 0))

    return pl.pallas_call(
        return_kernel,
        out_shape=(
            jax.ShapeDtypeStruct((tokens, width), f32),
            jax.ShapeDtypeStruct((tokens, 2 * width), bf16),
        ),
        grid_spec=pltpu.PrefetchScalarGridSpec(
            num_scalar_prefetch=1,
            grid=(tokens // BLOCK_K,),
            in_specs=[
                whole((tokens, width)),
                whole((tokens, width)),
                pl.BlockSpec((BLOCK_K, 2 * width), lambda i, b: (i, 0)),
                pl.BlockSpec((BLOCK_K, 1), lambda i, b: (i, 0)),
                whole((8, tokens)),
                whole((8, tokens)),
                whole((8, tokens)),
                whole((tokens, width)),
            ],
            out_specs=(
                whole((tokens, width)),
                pl.BlockSpec((BLOCK_K, 2 * width), lambda i, b: (i, 0)),
            ),
        ),
        name="attend_return",
    )(bounds, query, grad, kv_pair, seg_k, seg_q, lse, delta, dq)


def on_device(
    tokens,
    teacher,
    cotangent,
    doc_starts,
    doc_time,
    valid_mask,
    gain_one,
    bias_one,
    time_one,
    qkv_weight,
    out_weight,
    gain_two,
    bias_two,
    time_two,
    up_weight,
    up_bias,
    down_weight,
    down_bias,
):
    tok_rows = tokens.shape[1]
    width_d = tokens.shape[2]
    shards = lax.axis_size("shard")
    groups = lax.axis_size("hi")
    length = tok_rows * QUAD * groups
    quad_rows = QUAD * tok_rows
    part = LOCAL_HEADS * HEAD
    hi, lo = lax.axis_index("hi"), lax.axis_index("lo")
    core, shard = lax.axis_index("core"), lax.axis_index("shard")
    member = 2 * lo + core
    starts = doc_starts[0]
    slots = starts.shape[0]
    rows_w = qkv_weight.shape[0]

    def packed(time_weight, vectors):
        flat = jnp.concatenate([v.astype(bf16) for v in vectors])
        flat = jnp.pad(flat, (0, 16 * width_d - flat.shape[0]))
        return jnp.concatenate([time_weight, flat.reshape(16, width_d)], axis=0)

    stamp_high = (doc_time[0] // 8).astype(bf16)
    stamp_low = (doc_time[0] % 8).astype(bf16)
    pack_one = packed(time_one, [gain_one, bias_one, stamp_high, stamp_low])
    pack_two = packed(time_two, [gain_two, bias_two, down_bias, up_bias])

    def unpacked(gathered, sizes):
        blocks = gathered.reshape(shards, -1, width_d)
        time_full = blocks[:, :-16].reshape(TEMB, width_d)
        flat = blocks[:, -16:].reshape(shards, -1)
        pieces, at = [], 0
        for size in sizes:
            pieces.append(flat[:, at : at + size])
            at += size
        return time_full, pieces

    own_part = width_d // shards
    time_attn, (gain_attn, bias_attn, high_all, low_all) = unpacked(
        gather_shard(pack_one), [own_part, own_part, slots, slots]
    )
    gain_attn, bias_attn = gain_attn.reshape(-1), bias_attn.reshape(-1)
    stamps_all = high_all.astype(f32) * 8.0 + low_all.astype(f32)

    qkv_part = lax.dynamic_index_in_dim(
        qkv_weight.reshape(rows_w, 3, QUAD, part), member, 2, keepdims=False
    ).reshape(rows_w, 3 * part)
    qkv_own = gather_shard(qkv_part)

    time_mlp, (gain_mlp, bias_mlp, down_bias_full, up_bias_all) = unpacked(
        lax.all_gather(pack_two, "shard", axis=0, tiled=True),
        [own_part, own_part, own_part, up_bias.shape[0]],
    )
    gain_mlp, bias_mlp = gain_mlp.reshape(-1), bias_mlp.reshape(-1)
    down_bias_full = down_bias_full.reshape(-1)
    hidden_half = up_bias.shape[0] // 2
    up_bias_own = lax.dynamic_index_in_dim(
        up_bias_all.reshape(shards, 2, hidden_half), core, 1, keepdims=False
    ).reshape(-1)
    if shards == 2:
        out_own = lax.all_gather(half_of(out_weight, core), "shard", axis=0, tiled=True)
    else:
        out_all = lax.all_gather(out_weight, "shard", axis=0, tiled=True)
        out_own = lax.dynamic_index_in_dim(
            out_all.reshape(2, 2, part, width_d), core, 1, keepdims=False
        ).reshape(2 * part, width_d)
    up_part = lax.dynamic_index_in_dim(
        up_weight.reshape(rows_w, shards, 2, hidden_half), core, 2, keepdims=False
    ).reshape(rows_w, shards * hidden_half)
    up_own = lax.all_gather(up_part, "shard", axis=0, tiled=True)
    down_own = lax.all_gather(half_of(down_weight, core), "shard", axis=0, tiled=True)

    block_base = (hi * QUAD + member) * tok_rows
    quad_base = hi * quad_rows
    own_seg = segments_at(starts, block_base + jnp.arange(tok_rows, dtype=jnp.int32))
    one_hot = (own_seg[:, None] == jnp.arange(slots, dtype=jnp.int32)[None, :]).astype(bf16)
    features_all = time_features(stamps_all.reshape(-1)).astype(bf16).reshape(shards, slots, TEMB)
    features_docs = time_features(doc_time[0]).astype(bf16)
    features = times(one_hot, features_docs).astype(bf16)
    quad_places = quad_base + jnp.arange(quad_rows, dtype=jnp.int32)
    quad_seg = segments_at(starts, quad_places)
    offsets = quad_places - begins_at(starts, quad_places)
    cosine, signed_sine = turn_tables(offsets)
    seg_rows = jnp.concatenate(
        [
            segments_at(starts, quad_places - quad_rows)[None],
            quad_seg[None],
            segments_at(starts, quad_places + quad_rows)[None],
            jnp.zeros((5, quad_rows), jnp.int32),
        ],
        axis=0,
    )
    seg_columns = [seg_rows[k][:, None] for k in range(3)]

    valid = valid_mask[0].astype(f32)
    counted = jnp.full((8, LANES), jnp.sum(valid))
    for axis in ("core", "lo", "hi", "shard"):
        counted = sum_all(counted, axis)
    counted = counted[0, 0]

    block_in = tokens[0].astype(f32)
    act_pre, normed_one, scales_one, inv_one = norm_forward(
        block_in, gain_attn, bias_attn, features, time_attn
    )
    act_one = act_pre.astype(bf16)
    act_far = flip(act_one, "lo")
    act_pair = in_order(core, act_one, flip(act_one, "core"), 0)
    act_far = in_order(core, act_far, flip(act_far, "core"), 0)
    act_quad = in_order(lo, act_pair, act_far, 0)
    joined = times(act_quad, qkv_own)
    key_low = turn(joined[:, part : 2 * part], cosine, signed_sine).astype(bf16)
    kv_pair = jnp.concatenate([key_low, joined[:, 2 * part :].astype(bf16)], axis=1)
    up_pairs = [(i, i + 1) for i in range(groups - 1)]
    down_pairs = [(i + 1, i) for i in range(groups - 1)]
    kv_prev = lax.ppermute(kv_pair, "hi", up_pairs)
    kv_next = lax.ppermute(kv_pair, "hi", down_pairs)
    query_low = (turn(joined[:, :part], cosine, signed_sine) * (LOG2E * HEAD**-0.5)).astype(bf16)

    def ranges(row_shift, row_block, col_shift, col_block):
        return block_ranges(
            starts,
            length,
            quad_base + row_shift,
            row_block,
            quad_base + col_shift,
            col_block,
            quad_rows,
        )

    acc, stat = attend_near(
        ranges(0, BLOCK_Q, 0, BLOCK_K), query_low, kv_pair, seg_columns[1], seg_rows
    )
    mixed_quad, lse = attend_far(
        ranges(0, BLOCK_Q, -quad_rows, BLOCK_K),
        ranges(0, BLOCK_Q, quad_rows, BLOCK_K),
        query_low,
        kv_prev,
        kv_next,
        seg_columns[1],
        seg_rows,
        acc,
        stat,
    )

    def to_chip(value):
        kept, sent = half_of(value, lo), half_of(value, 1 - lo)
        return in_order(lo, kept, flip(sent, "lo"), 1)

    def to_quad(value):
        left, right = value[:, :part], value[:, part:]
        kept = jnp.where(lo == 0, left, right)
        sent = jnp.where(lo == 0, right, left)
        return in_order(lo, kept, flip(sent, "lo"), 0)

    def both_cores(value):
        return in_order(core, value, flip(value, "core"), 0)

    def own_tokens(partial):
        sent = flip(half_of(partial, 1 - core).astype(bf16), "core")
        return half_of(partial, core) + sent.astype(f32)

    mixed_low = to_chip(mixed_quad)
    middle = block_in + own_tokens(times(mixed_low, out_own))

    act_pre_two, normed_two, scales_two, inv_two = norm_forward(
        middle, gain_mlp, bias_mlp, features, time_mlp
    )
    act_two = both_cores(act_pre_two.astype(bf16))
    upper_in = times(act_two, up_own) + up_bias_own.astype(f32)[None, :]
    normal_cdf = 0.5 + 0.5 * lax.erf(upper_in * math.sqrt(0.5))
    density = jnp.exp(-0.5 * upper_in * upper_in) * (1.0 / math.sqrt(2.0 * math.pi))
    hidden = (upper_in * normal_cdf).astype(bf16)
    slope = (normal_cdf + upper_in * density).astype(bf16)
    block_out = (
        middle + own_tokens(times(hidden, down_own)) + down_bias_full.astype(f32)[None, :]
    )
    misfit = block_out - teacher[0].astype(f32)
    square_sum = jnp.sum(valid[:, None] * misfit * misfit)
    grad_final = (
        cotangent[0].astype(f32) + 2.0 / (counted * width_d) * valid[:, None] * misfit
    )
    grad_mid_own = grad_final.astype(bf16)
    grad_mid = both_cores(grad_mid_own)
    grad_down = contract_rows(hidden, grad_mid)
    grad_down_bias = jnp.sum(grad_mid_own.astype(f32), axis=0, keepdims=True)
    grad_upper = (times_trans(grad_mid, down_own) * slope.astype(f32)).astype(bf16)
    grad_up = contract_rows(act_two, grad_upper)
    grad_up_bias = jnp.sum(grad_upper.astype(f32), axis=0)
    grad_act_two = own_tokens(times_trans(grad_upper, up_own))
    grad_in_two, grad_gain_two, grad_bias_two, by_doc_two = norm_backward(
        grad_act_two, normed_two, scales_two, inv_two, one_hot
    )
    grad_middle = grad_final + grad_in_two
    grad_branch = both_cores(grad_middle.astype(bf16))
    grad_mixed = times_trans(grad_branch, out_own).astype(bf16)
    grad_out = contract_rows(mixed_low, grad_branch)

    if shards == 2:
        out_rows = grad_out
    else:
        by_core = lax.all_gather(grad_out.astype(bf16), "core", axis=0, tiled=False)
        out_rows = jnp.transpose(
            by_core.reshape(2, 2, part, width_d), (1, 0, 2, 3)
        ).reshape(2 * 2 * part, width_d)
    blocks = [
        grad_down.astype(bf16).reshape(shards, -1, width_d),
        grad_up.astype(bf16).reshape(shards, -1, width_d),
        out_rows.astype(bf16).reshape(shards, -1, width_d),
    ]
    sizes = [b.shape[1] for b in blocks]
    pairs = 2 * groups
    pieces = jnp.concatenate(
        [b.reshape(shards, pairs, -1, width_d) for b in blocks], axis=2
    ).reshape(-1, width_d)
    reduced = lax.psum_scatter(pieces, ("shard", "hi", "lo"), scatter_dimension=0, tiled=True)
    everyone = lax.all_gather(reduced, ("hi", "lo", "core"), axis=0, tiled=True)
    everyone = everyone.reshape(pairs, 2, -1, width_d)
    cut = [0]
    for size in sizes:
        cut.append(cut[-1] + size // pairs)

    def of_block(k):
        return jnp.transpose(everyone[:, :, cut[k] : cut[k + 1]], (1, 0, 2, 3)).reshape(
            2, sizes[k], width_d
        )

    down_total = of_block(0).reshape(2 * sizes[0], width_d).astype(f32)
    up_total = (
        jnp.transpose(of_block(1).reshape(2, rows_w, shards, hidden_half), (1, 2, 0, 3))
        .reshape(rows_w, shards * 2 * hidden_half)
        .astype(f32)
    )
    if shards == 2:
        out_total = of_block(2).reshape(2 * sizes[2], width_d).astype(f32)
    else:
        out_total = of_block(2)[0].astype(f32)

    grad_quad = to_quad(grad_mixed)
    head_of = jnp.arange(part, dtype=jnp.int32) // HEAD
    summing = (jnp.arange(8, dtype=jnp.int32)[:, None] == head_of[None, :]).astype(f32)
    delta = lax.dot_general(
        summing,
        grad_quad.astype(f32) * mixed_quad.astype(f32),
        (((1,), (1,)), ((), ())),
        precision=lax.Precision.HIGHEST,
        preferred_element_type=f32,
    )
    seg_q_rows = jnp.broadcast_to(quad_seg[None], (8, quad_rows))

    def give_back(row_shift, kv, k, dq):
        return attend_return(
            ranges(row_shift, BLOCK_K, 0, BLOCK_Q),
            query_low,
            grad_quad,
            kv,
            seg_columns[k],
            seg_q_rows,
            lse,
            delta,
            dq,
        )

    dq, dkv_prev = give_back(-quad_rows, kv_prev, 0, jnp.zeros((quad_rows, part), f32))
    from_next = lax.ppermute(dkv_prev, "hi", down_pairs)
    dq, dkv_next = give_back(quad_rows, kv_next, 2, dq)
    from_prev = lax.ppermute(dkv_next, "hi", up_pairs)
    dq, dkv_own = give_back(0, kv_pair, 1, dq)
    dkv = dkv_own.astype(f32) + from_next.astype(f32) + from_prev.astype(f32)
    grad_joined = jnp.concatenate(
        [
            turn(dq * HEAD**-0.5, cosine, -signed_sine),
            turn(dkv[:, :part], cosine, -signed_sine),
            dkv[:, part:],
        ],
        axis=1,
    ).astype(bf16)

    partial_act = times_trans(grad_joined, qkv_own)
    far_act = flip(half_of(partial_act, 1 - lo).astype(bf16), "lo")
    grad_act_one = own_tokens(half_of(partial_act, lo) + far_act.astype(f32))
    grad_qkv = contract_rows(act_quad, grad_joined)
    grad_in_one, grad_gain_one, grad_bias_one, by_doc_one = norm_backward(
        grad_act_one, normed_one, scales_one, inv_one, one_hot
    )
    input_grad = grad_middle + grad_in_one

    qkv_rows = scatter_sum(scatter_sum(grad_qkv, "shard"), "hi").astype(bf16)
    qkv_rows = gather_back(qkv_rows, "hi").reshape(1, rows_w, 3 * part)
    qkv_rows = gather_back(gather_back(qkv_rows, "core"), "lo")
    qkv_total = (
        jnp.transpose(qkv_rows.reshape(QUAD, rows_w, 3, part), (1, 2, 0, 3))
        .reshape(rows_w, 3 * QUAD * part)
        .astype(f32)
    )

    bias_slots = jnp.where(
        jnp.arange(2, dtype=jnp.int32)[None, :, None] == core,
        grad_up_bias.reshape(shards, 1, hidden_half),
        0.0,
    ).reshape(-1, width_d)
    summed_rows = [grad_gain_one, grad_bias_one, grad_gain_two, grad_bias_two, grad_down_bias]
    small = jnp.concatenate(
        summed_rows + [bias_slots, jnp.full((1, width_d), square_sum), by_doc_one, by_doc_two],
        axis=0,
    )
    filled = small.shape[0]
    small = jnp.pad(small, ((0, -filled % 8), (0, 0)))
    for axis in ("hi", "lo", "core"):
        small = sum_all(small, axis)
    small_all = gather_shard(small).reshape(shards, -1, width_d)
    bias_rows = bias_slots.shape[0]
    head_rows = 6 + bias_rows
    totals = jnp.sum(small_all[:, :head_rows], axis=0)
    docs_one = small_all[:, head_rows : head_rows + slots]
    docs_two = small_all[:, head_rows + slots : head_rows + 2 * slots]

    def own_vector(row):
        return lax.dynamic_slice_in_dim(row, shard * own_part, own_part, 0)

    own_features = lax.dynamic_slice_in_dim(
        features_all, shard * (TEMB // shards), TEMB // shards, 2
    ).astype(f32)

    def time_total(docs):
        return lax.dot_general(
            own_features,
            docs,
            (((0, 1), (0, 1)), ((), ())),
            precision=lax.Precision.HIGHEST,
            preferred_element_type=f32,
        )

    up_bias_total = lax.dynamic_slice_in_dim(
        totals[5 : 5 + bias_rows].reshape(-1), shard * 2 * hidden_half, 2 * hidden_half, 0
    )
    loss_value = totals[5 + bias_rows, 0] / (counted * width_d)
    return (
        block_out.astype(bf16)[None],
        loss_value,
        input_grad[None],
        own_vector(totals[0]),
        own_vector(totals[1]),
        time_total(docs_one),
        qkv_total,
        out_total,
        own_vector(totals[2]),
        own_vector(totals[3]),
        time_total(docs_two),
        up_total,
        up_bias_total,
        down_total,
        own_vector(totals[4]),
    )


def solution(mesh):
    ctx, shards = mesh.shape["ctx"], mesh.shape["shard"]
    fine = Mesh(
        mesh.devices.reshape(ctx // QUAD, 2, 2, shards), ("hi", "lo", "core", "shard")
    )
    blocks = ("hi", "lo", "core")
    in_specs = (
        P("shard", blocks, None),
        P("shard", blocks, None),
        P("shard", blocks, None),
        P("shard", None),
        P("shard", None),
        P("shard", blocks),
        P("shard"),
        P("shard"),
        P("shard", None),
        P("shard", None),
        P("shard", None),
        P("shard"),
        P("shard"),
        P("shard", None),
        P("shard", None),
        P("shard"),
        P("shard", None),
        P("shard"),
    )
    out_specs = (
        P("shard", blocks, None),
        P(),
        P("shard", blocks, None),
        P("shard"),
        P("shard"),
        P("shard", None),
        P("shard", None),
        P("shard", None),
        P("shard"),
        P("shard"),
        P("shard", None),
        P("shard", None),
        P("shard"),
        P("shard", None),
        P("shard"),
    )
    return jax.shard_map(
        on_device, mesh=fine, in_specs=in_specs, out_specs=out_specs, check_vma=False
    )
```

```python
import math

import jax
import jax.numpy as jnp
from jax import lax
from jax.experimental import pallas as pl
from jax.experimental.pallas import tpu as pltpu
from jax.sharding import Mesh
from jax.sharding import PartitionSpec as P

HEADS = 16
HEAD = 64
TEMB = 256
QUAD = 4
LOCAL_HEADS = HEADS // QUAD
LANES = 128
BLOCK_Q = 512
BLOCK_K = 512
norm_eps = 1e-05
masked_value = -1e30
LOG2E = math.log2(math.e)
bf16 = jnp.bfloat16
f32 = jnp.float32


def flip(value, axis):
    return lax.ppermute(value, axis, [(0, 1), (1, 0)])


def in_order(index, own, other, axis):
    return jnp.where(
        index == 0,
        jnp.concatenate([own, other], axis=axis),
        jnp.concatenate([other, own], axis=axis),
    )


def half_of(value, index):
    rows = value.shape[0] // 2
    return lax.dynamic_slice_in_dim(value, index * rows, rows, 0)


def xor_pairs(size, bit):
    return [(i, i ^ bit) for i in range(size)]


def bits_of(axis):
    return [1 << b for b in range(lax.axis_size(axis).bit_length() - 1)]


def scatter_sum(value, axis, bits):
    size = lax.axis_size(axis)
    for bit in bits:
        mine = (lax.axis_index(axis) // bit) % 2
        sent = half_of(value, 1 - mine).astype(bf16)
        got = lax.ppermute(sent, axis, xor_pairs(size, bit))
        value = half_of(value, mine).astype(f32) + got.astype(f32)
    return value


def gather_back(value, axis):
    size = lax.axis_size(axis)
    for bit in reversed(bits_of(axis)):
        got = lax.ppermute(value, axis, xor_pairs(size, bit))
        value = jnp.concatenate([value, got], axis=0)
    return value


def sum_all(value, axis, bits):
    size = lax.axis_size(axis)
    for bit in bits:
        value = value + lax.ppermute(value, axis, xor_pairs(size, bit))
    return value


def gather_shard(value):
    if lax.axis_size("shard") == 2:
        return in_order(lax.axis_index("shard"), value, flip(value, "shard"), 0)
    return lax.all_gather(value, "shard", axis=0, tiled=True)


def contract_rows(left_side, right_side):
    return lax.dot_general(
        left_side, right_side, (((0,), (0,)), ((), ())), preferred_element_type=f32
    )


def times_trans(left_side, right_side):
    return lax.dot_general(
        left_side, right_side, (((1,), (1,)), ((), ())), preferred_element_type=f32
    )


def times(left_side, right_side):
    return jnp.dot(left_side, right_side, preferred_element_type=f32)


def segments_at(starts, places):
    return jnp.sum((starts[None, :] <= places[:, None]).astype(jnp.int32), axis=1) - 1


def begins_at(starts, places):
    return jnp.max(jnp.where(starts[None, :] <= places[:, None], starts[None, :], 0), axis=1)


def ends_at(starts, places, length):
    return jnp.min(jnp.where(starts[None, :] > places[:, None], starts[None, :], length), axis=1)


def block_ranges(starts, length, row_base, row_block, col_base, col_block, tokens):
    count = tokens // row_block
    first = row_base + row_block * jnp.arange(count, dtype=jnp.int32)
    last = first + row_block - 1
    real = jnp.logical_and(first >= 0, last < length)
    begin_first = begins_at(starts, first)
    low = jnp.clip(begin_first - col_base, 0, tokens)
    high = jnp.clip(ends_at(starts, last, length) - col_base, 0, tokens)
    live = jnp.logical_and(real, high > low)
    low_block = jnp.where(live, low // col_block, 0)
    high_block = jnp.where(live, (high + col_block - 1) // col_block, 0)
    whole = jnp.logical_and(live, begin_first == begins_at(starts, last))
    full_low = jnp.where(whole, (low + col_block - 1) // col_block, high_block)
    full_high = jnp.where(whole, high // col_block, high_block)
    full_low = jnp.minimum(full_low, high_block)
    full_high = jnp.clip(full_high, full_low, high_block)
    return jnp.stack([low_block, full_low, full_high, high_block]).astype(jnp.int32)


def time_features(time_index):
    halfway = TEMB // 2
    ladder = jnp.exp(-math.log(10000.0) * jnp.arange(halfway, dtype=f32) / halfway)
    phases = time_index.astype(f32)[:, None] * ladder[None, :]
    return jnp.concatenate([jnp.sin(phases), jnp.cos(phases)], axis=1)


def turn_tables(places):
    halfway = HEAD // 2
    ladder = jnp.exp(-math.log(10000.0) * 2.0 * jnp.arange(halfway, dtype=f32) / HEAD)
    turned = places.astype(f32)[:, None] * jnp.tile(ladder, LANES // halfway)[None, :]
    sign = jnp.where(jnp.arange(LANES) % HEAD < halfway, -1.0, 1.0).astype(f32)
    return jnp.cos(turned), jnp.sin(turned) * sign[None, :]


def norm_forward(values, gain_vec, bias_vec, features, time_weight):
    average = jnp.mean(values, axis=1, keepdims=True)
    centred = values - average
    inv_std = lax.rsqrt(jnp.mean(centred * centred, axis=1, keepdims=True) + norm_eps)
    normed = centred * inv_std
    scales = gain_vec.astype(f32)[None, :] + times(features, time_weight)
    return (normed * scales + bias_vec.astype(f32)[None, :], normed, scales, inv_std)


def norm_backward(grad_act, normed, scales, inv_std, one_hot):
    grad_scale = grad_act * normed
    grad_gain = jnp.sum(grad_scale, axis=0, keepdims=True)
    grad_bias = jnp.sum(grad_act, axis=0, keepdims=True)
    by_doc = contract_rows(one_hot, grad_scale.astype(bf16))
    grad_norm = grad_act * scales
    grad_input = inv_std * (
        grad_norm
        - jnp.mean(grad_norm, axis=1, keepdims=True)
        - normed * jnp.mean(grad_norm * normed, axis=1, keepdims=True)
    )
    return (grad_input, grad_gain, grad_bias, by_doc)


def pick_kernel(picks, weight_ref, out_ref):
    out_ref[...] = weight_ref[...]


def pick_columns(weight, picks, block):
    rows, count = weight.shape[0], picks.shape[0]
    return pl.pallas_call(
        pick_kernel,
        out_shape=jax.ShapeDtypeStruct((rows, count * block), weight.dtype),
        grid_spec=pltpu.PrefetchScalarGridSpec(
            num_scalar_prefetch=1,
            grid=(count,),
            in_specs=[pl.BlockSpec((rows, block), lambda i, p: (0, p[i]))],
            out_specs=pl.BlockSpec((rows, block), lambda i, p: (0, i)),
        ),
        cost_estimate=pl.CostEstimate(
            flops=0, transcendentals=0, bytes_accessed=4 * rows * count * block
        ),
        name="pick_columns",
    )(picks, weight)


def assemble_kernel(core, down_ref, up_ref, out_ref):
    early = pl.program_id(0) < pl.num_programs(0) // 2
    out_ref[...] = jnp.where(early, down_ref[...], up_ref[...])


def assemble(down, up, core):
    wide, rows = down.shape[1], up.shape[0]
    count = down.shape[0] // 2 // rows
    return pl.pallas_call(
        assemble_kernel,
        out_shape=jax.ShapeDtypeStruct((2 * count * rows, wide), down.dtype),
        grid_spec=pltpu.PrefetchScalarGridSpec(
            num_scalar_prefetch=1,
            grid=(2 * count,),
            in_specs=[
                pl.BlockSpec(
                    (rows, wide), lambda i, core: (core[0] * count + jnp.minimum(i, count - 1), 0)
                ),
                pl.BlockSpec(
                    (rows, wide), lambda i, core: (0, 2 * jnp.maximum(i - count, 0) + core[0])
                ),
            ],
            out_specs=pl.BlockSpec((rows, wide), lambda i, core: (i, 0)),
        ),
        cost_estimate=pl.CostEstimate(
            flops=0, transcendentals=0, bytes_accessed=6 * down.size
        ),
        name="assemble",
    )(core, down, up)


def lane_halves(value):
    lane = lax.broadcasted_iota(jnp.int32, value.shape, 1)
    zero = jnp.zeros_like(value)
    return jnp.where(lane < HEAD, value, zero), jnp.where(lane < HEAD, zero, value)


def within(reach, first, side):
    begins, ends = reach
    place = lax.broadcasted_iota(jnp.int32, (BLOCK_K, BLOCK_Q), 0)
    if side < 0:
        return place >= begins - first
    if side > 0:
        return place < ends - first
    return jnp.logical_and(place >= begins - first, place < ends - first)


def look_through(bounds, step, queries, kv_ref, pair, reach, base, where, state):
    def visit(masked):
        def body(block, carried):
            rows = pl.ds(pl.multiple_of(block * BLOCK_K, BLOCK_K), BLOCK_K)
            keys = kv_ref[rows, pair * LANES : (pair + 1) * LANES]
            if masked:
                allowed = within(reach, base + block * BLOCK_K, where)
            after = []
            for side in range(2):
                top_old, total_old, acc_old = carried[side]
                value_lane = LOCAL_HEADS * HEAD + (2 * pair + side) * HEAD
                values = kv_ref[rows, value_lane : value_lane + HEAD]
                scores = times_trans(keys, queries[side])
                if masked:
                    scores = jnp.where(allowed, scores, masked_value)
                top = jnp.maximum(top_old, jnp.max(scores, axis=0, keepdims=True))
                weights = jnp.exp2(scores - top)
                scale = jnp.exp2(top_old - top)
                total = total_old * scale + jnp.sum(weights, axis=0, keepdims=True)
                acc = acc_old * scale + contract_rows(values, weights.astype(bf16))
                after.append((top, total, acc))
            return tuple(after)

        return body

    low, full_low, full_high, high = (bounds[k, step] for k in range(4))
    state = lax.fori_loop(low, full_low, visit(True), state)
    state = lax.fori_loop(full_low, full_high, visit(False), state)
    return lax.fori_loop(full_high, high, visit(True), state)


def near_kernel(bounds, query_ref, kv_ref, reach_ref, acc_ref, stat_ref):
    step = pl.program_id(0)
    reach = (reach_ref[0:1, :], reach_ref[1:2, :])
    for pair in range(LOCAL_HEADS // 2):
        queries = lane_halves(query_ref[:, pair * LANES : (pair + 1) * LANES])
        top = jnp.full((1, BLOCK_Q), masked_value, f32)
        total = jnp.zeros((1, BLOCK_Q), f32)
        acc = jnp.zeros((HEAD, BLOCK_Q), f32)
        state = ((top, total, acc), (top, total, acc))
        state = look_through(bounds, step, queries, kv_ref, pair, reach, 0, 0, state)
        for side in range(2):
            head = 2 * pair + side
            stat_ref[head : head + 1, :] = state[side][0]
            stat_ref[LOCAL_HEADS + head : LOCAL_HEADS + head + 1, :] = state[side][1]
            acc_ref[head * HEAD : (head + 1) * HEAD, :] = state[side][2]


def far_kernel(
    before,
    after,
    query_ref,
    prev_ref,
    next_ref,
    reach_ref,
    acc_in,
    stat_in,
    out_ref,
    lse_ref,
):
    step = pl.program_id(0)
    tokens = prev_ref.shape[0]
    reach = (reach_ref[0:1, :], reach_ref[1:2, :])
    lse_ref[...] = jnp.zeros_like(lse_ref)
    mixed = []
    for pair in range(LOCAL_HEADS // 2):
        queries = lane_halves(query_ref[:, pair * LANES : (pair + 1) * LANES])
        state = tuple(
            (
                stat_in[head : head + 1, :],
                stat_in[LOCAL_HEADS + head : LOCAL_HEADS + head + 1, :],
                acc_in[head * HEAD : (head + 1) * HEAD, :],
            )
            for head in (2 * pair, 2 * pair + 1)
        )
        state = look_through(before, step, queries, prev_ref, pair, reach, -tokens, -1, state)
        state = look_through(after, step, queries, next_ref, pair, reach, tokens, 1, state)
        for side in range(2):
            top, total, acc = state[side]
            head = 2 * pair + side
            lse_ref[head : head + 1, :] = top + jnp.log2(total)
            mixed.append(acc / total)
    out_ref[...] = jnp.transpose(jnp.concatenate(mixed, axis=0)).astype(out_ref.dtype)


def whole(shape):
    return pl.BlockSpec(shape, lambda i, *_: (0,) * len(shape))


def guess(tokens, width, matmuls):
    work = 2 * tokens * (tokens // 2) * width * matmuls * 3
    return pl.CostEstimate(
        flops=work, transcendentals=tokens * tokens * LOCAL_HEADS // 2, bytes_accessed=8 * tokens * width
    )


def attend_near(bounds, query, kv_pair, reach):
    tokens, width = query.shape
    return pl.pallas_call(
        near_kernel,
        out_shape=(
            jax.ShapeDtypeStruct((width, tokens), f32),
            jax.ShapeDtypeStruct((8, tokens), f32),
        ),
        grid_spec=pltpu.PrefetchScalarGridSpec(
            num_scalar_prefetch=1,
            grid=(tokens // BLOCK_Q,),
            in_specs=[
                pl.BlockSpec((BLOCK_Q, width), lambda i, b: (i, 0)),
                whole((tokens, 2 * width)),
                pl.BlockSpec((8, BLOCK_Q), lambda i, b: (0, i)),
            ],
            out_specs=(
                pl.BlockSpec((width, BLOCK_Q), lambda i, b: (0, i)),
                pl.BlockSpec((8, BLOCK_Q), lambda i, b: (0, i)),
            ),
        ),
        cost_estimate=guess(tokens, width, 4),
        name="attend_near",
    )(bounds, query, kv_pair, reach)


def attend_far(before, after, query, kv_prev, kv_next, reach, acc, stat):
    tokens, width = query.shape
    return pl.pallas_call(
        far_kernel,
        out_shape=(
            jax.ShapeDtypeStruct((tokens, width), bf16),
            jax.ShapeDtypeStruct((8, tokens), f32),
        ),
        grid_spec=pltpu.PrefetchScalarGridSpec(
            num_scalar_prefetch=2,
            grid=(tokens // BLOCK_Q,),
            in_specs=[
                pl.BlockSpec((BLOCK_Q, width), lambda i, b, a: (i, 0)),
                whole((tokens, 2 * width)),
                whole((tokens, 2 * width)),
                pl.BlockSpec((8, BLOCK_Q), lambda i, b, a: (0, i)),
                pl.BlockSpec((width, BLOCK_Q), lambda i, b, a: (0, i)),
                pl.BlockSpec((8, BLOCK_Q), lambda i, b, a: (0, i)),
            ],
            out_specs=(
                pl.BlockSpec((BLOCK_Q, width), lambda i, b, a: (i, 0)),
                pl.BlockSpec((8, BLOCK_Q), lambda i, b, a: (0, i)),
            ),
        ),
        cost_estimate=guess(tokens, width, 2),
        name="attend_far",
    )(before, after, query, kv_prev, kv_next, reach, acc, stat)


def return_kernel(first, shift, bounds, query_ref, grad_ref, kv_ref, reach_ref, lse_ref, delta_ref, *refs):
    dq_ref, dkv_ref = refs[-2:]
    step = pl.program_id(0)
    width = LOCAL_HEADS * HEAD

    @pl.when(step == 0)
    def _():
        dq_ref[...] = jnp.zeros_like(dq_ref) if first else refs[0][...]

    low, full_low, full_high, high = (bounds[k, step] for k in range(4))
    for pair in range(LOCAL_HEADS // 2):
        lanes = slice(pair * LANES, (pair + 1) * LANES)
        keys = lane_halves(kv_ref[:, lanes])
        values = lane_halves(kv_ref[:, width + pair * LANES : width + (pair + 1) * LANES])
        keys_t = jnp.transpose(kv_ref[:, lanes].astype(f32)).astype(bf16)

        def visit(masked, pair=pair, lanes=lanes, keys=keys, values=values, keys_t=keys_t):
            def body(block, carried):
                dk, dv = carried
                rows = pl.ds(pl.multiple_of(block * BLOCK_Q, BLOCK_Q), BLOCK_Q)
                query_pair = query_ref[rows, lanes]
                grad_pair = grad_ref[rows, lanes]
                queries = lane_halves(query_pair)
                grads = lane_halves(grad_pair)
                if masked:
                    reach = (reach_ref[0:1, rows], reach_ref[1:2, rows])
                    allowed = within(reach, shift + step * BLOCK_K, shift)
                for side in range(2):
                    head = 2 * pair + side
                    scores = times_trans(keys[side], query_pair) - lse_ref[head : head + 1, rows]
                    if masked:
                        scores = jnp.where(allowed, scores, masked_value)
                    prob = jnp.exp2(scores)
                    grad_prob = times_trans(values[side], grad_pair) - delta_ref[head : head + 1, rows]
                    grad_scores = (prob * grad_prob).astype(bf16)
                    dv = dv + times(prob.astype(bf16), grads[side])
                    dk = dk + times(grad_scores, queries[side])
                    head_rows = slice(head * HEAD, (head + 1) * HEAD)
                    dq_ref[head_rows, rows] += times(
                        keys_t[side * HEAD : (side + 1) * HEAD], grad_scores
                    )
                return dk, dv

            return body

        start = jnp.zeros((BLOCK_K, LANES), f32)
        state = lax.fori_loop(low, full_low, visit(True), (start, start))
        state = lax.fori_loop(full_low, full_high, visit(False), state)
        dk, dv = lax.fori_loop(full_high, high, visit(True), state)
        dkv_ref[:, lanes] = (dk * (1.0 / LOG2E)).astype(dkv_ref.dtype)
        dkv_ref[:, width + pair * LANES : width + (pair + 1) * LANES] = dv.astype(dkv_ref.dtype)


def attend_return(shift, bounds, query, grad, kv_pair, reach, lse, delta, dq):
    tokens, width = query.shape
    first = dq is None
    specs = [
        whole((tokens, width)),
        whole((tokens, width)),
        pl.BlockSpec((BLOCK_K, 2 * width), lambda i, b: (i, 0)),
        whole((8, tokens)),
        whole((8, tokens)),
        whole((8, tokens)),
    ]
    operands = [bounds, query, grad, kv_pair, reach, lse, delta]
    if not first:
        specs.append(whole((width, tokens)))
        operands.append(dq)

    def kernel(*refs):
        return_kernel(first, shift, *refs)

    return pl.pallas_call(
        kernel,
        out_shape=(
            jax.ShapeDtypeStruct((width, tokens), f32),
            jax.ShapeDtypeStruct((tokens, 2 * width), bf16),
        ),
        grid_spec=pltpu.PrefetchScalarGridSpec(
            num_scalar_prefetch=1,
            grid=(tokens // BLOCK_K,),
            in_specs=specs,
            out_specs=(
                whole((width, tokens)),
                pl.BlockSpec((BLOCK_K, 2 * width), lambda i, b: (i, 0)),
            ),
        ),
        cost_estimate=guess(tokens, width, 5),
        name="attend_return",
    )(*operands)


def project_kernel(
    places,
    own_ref,
    other_ref,
    feature_ref,
    time_ref,
    vector_ref,
    left_ref,
    right_ref,
    cosine_ref,
    sine_ref,
    *refs,
):
    act_ref, query_ref, kv_ref = refs[-3:]
    width = query_ref.shape[1]
    early = pl.program_id(0) < pl.num_programs(0) // 2
    values = jnp.where(early, own_ref[...], other_ref[...]).astype(f32)
    average = jnp.mean(values, axis=1, keepdims=True)
    centred = values - average
    inv_std = lax.rsqrt(jnp.mean(centred * centred, axis=1, keepdims=True) + norm_eps)
    scales = vector_ref[0:1, :] + times(feature_ref[...], time_ref[...])
    act_ref[...] = (centred * inv_std * scales + vector_ref[1:2, :]).astype(bf16)
    half = left_ref.shape[0]
    first = pl.multiple_of(places[1] * half, half)
    second = pl.multiple_of((1 - places[1]) * half, half)
    joined = times(act_ref[:, pl.ds(first, half)], left_ref[...]) + times(
        act_ref[:, pl.ds(second, half)], right_ref[...]
    )
    cosine = jnp.concatenate([cosine_ref[...]] * (width // LANES), axis=1)
    sine = jnp.concatenate([sine_ref[...]] * (width // LANES), axis=1)
    query = turn_lanes(joined[:, :width], cosine, sine)
    query_ref[...] = (query * (LOG2E * HEAD**-0.5)).astype(bf16)
    kv_ref[:, :width] = turn_lanes(joined[:, width : 2 * width], cosine, sine).astype(bf16)
    kv_ref[:, width:] = joined[:, 2 * width :].astype(bf16)


def turn_lanes(vectors, cosine, signed_sine):
    halfway = HEAD // 2
    lane = lax.broadcasted_iota(jnp.int32, vectors.shape, 1) % HEAD
    from_right = pltpu.roll(vectors, vectors.shape[1] - halfway, 1)
    from_left = pltpu.roll(vectors, halfway, 1)
    return vectors * cosine + jnp.where(lane < halfway, from_right, from_left) * signed_sine


def project(places, own, other, features, time_full, vectors, left, right, cosine, sine, before):
    rows, wide = own.shape
    width = left.shape[1] // 3
    step = min(rows, 256)
    count = rows // step

    def placed(columns):
        return pl.BlockSpec(
            (step, columns),
            lambda i, places: ((places[0] ^ (i // count)) * count + i % count, 0),
        )

    in_specs = [
        pl.BlockSpec((step, wide), lambda i, places: (jnp.minimum(i, count - 1), 0)),
        pl.BlockSpec((step, wide), lambda i, places: (jnp.maximum(i - count, 0), 0)),
        placed(TEMB),
        whole(time_full.shape),
        whole(vectors.shape),
        whole(left.shape),
        whole(right.shape),
        placed(LANES),
        placed(LANES),
    ]
    operands = [own, other, features, time_full, vectors, left, right, cosine, sine]
    aliases = {}
    if before is not None:
        for k, array in enumerate(before):
            aliases[1 + len(operands)] = k
            operands.append(array)
            in_specs.append(pl.BlockSpec(memory_space=pl.ANY))
    return pl.pallas_call(
        project_kernel,
        out_shape=(
            jax.ShapeDtypeStruct((QUAD * rows, wide), bf16),
            jax.ShapeDtypeStruct((QUAD * rows, width), bf16),
            jax.ShapeDtypeStruct((QUAD * rows, 2 * width), bf16),
        ),
        grid_spec=pltpu.PrefetchScalarGridSpec(
            num_scalar_prefetch=1,
            grid=(2 * count,),
            in_specs=in_specs,
            out_specs=(placed(wide), placed(width), placed(2 * width)),
        ),
        input_output_aliases=aliases,
        cost_estimate=pl.CostEstimate(
            flops=4 * rows * wide * 4 * width, transcendentals=0, bytes_accessed=16 * rows * wide
        ),
        name="project",
    )(places, *operands)


def unproject_kernel(
    places,
    dq_ref,
    own_ref,
    next_ref,
    prev_ref,
    cosine_ref,
    sine_ref,
    act_ref,
    weight_ref,
    send_ref,
    keep_ref,
    grad_send_ref,
    grad_keep_ref,
    grad_acc,
):
    step, steps = pl.program_id(0), pl.num_programs(0)
    width = dq_ref.shape[0]
    cosine = jnp.concatenate([cosine_ref[...]] * (width // LANES), axis=1)
    sine = jnp.concatenate([sine_ref[...]] * (width // LANES), axis=1)
    dkv = own_ref[...].astype(f32) + next_ref[...].astype(f32) + prev_ref[...].astype(f32)
    dq = jnp.transpose(dq_ref[...]) * HEAD**-0.5
    grad_joined = jnp.concatenate(
        [
            turn_lanes(dq, cosine, -sine).astype(bf16),
            turn_lanes(dkv[:, :width], cosine, -sine).astype(bf16),
            dkv[:, width:].astype(bf16),
        ],
        axis=1,
    )
    partial_act = times_trans(grad_joined, weight_ref[...])

    @pl.when(step < steps // 2)
    def _():
        send_ref[...] = partial_act.astype(bf16)

    @pl.when(step >= steps // 2)
    def _():
        keep_ref[...] = partial_act

    grad = contract_rows(act_ref[...], grad_joined)

    @pl.when(step == 0)
    def _():
        grad_acc[...] = grad

    @pl.when(step > 0)
    def _():
        grad_acc[...] += grad

    @pl.when(step == steps - 1)
    def _():
        half = grad_acc.shape[0] // 2
        sent = pl.multiple_of((1 - places[1]) * half, half)
        kept = pl.multiple_of(places[1] * half, half)
        grad_send_ref[...] = grad_acc[pl.ds(sent, half), :].astype(bf16)
        grad_keep_ref[...] = grad_acc[pl.ds(kept, half), :]


def unproject(places, dq, own, after, before, cosine, sine, act, weight):
    width, rows = dq.shape
    wide = act.shape[1]
    steps = 4
    step = rows // steps

    def order(i, places):
        return (i + (1 - places[0]) * (steps // 2)) % steps

    def rowed(columns):
        return pl.BlockSpec((step, columns), lambda i, places: (order(i, places), 0))

    return pl.pallas_call(
        unproject_kernel,
        out_shape=(
            jax.ShapeDtypeStruct((rows // 2, wide), bf16),
            jax.ShapeDtypeStruct((rows // 2, wide), f32),
            jax.ShapeDtypeStruct((wide // 2, 3 * width), bf16),
            jax.ShapeDtypeStruct((wide // 2, 3 * width), f32),
        ),
        grid_spec=pltpu.PrefetchScalarGridSpec(
            num_scalar_prefetch=1,
            grid=(steps,),
            in_specs=[
                pl.BlockSpec((width, step), lambda i, places: (0, order(i, places))),
                rowed(2 * width),
                rowed(2 * width),
                rowed(2 * width),
                rowed(LANES),
                rowed(LANES),
                rowed(wide),
                whole(weight.shape),
            ],
            out_specs=(
                pl.BlockSpec((step, wide), lambda i, places: (jnp.minimum(i, steps // 2 - 1), 0)),
                pl.BlockSpec((step, wide), lambda i, places: (jnp.maximum(i - steps // 2, 0), 0)),
                whole((wide // 2, 3 * width)),
                whole((wide // 2, 3 * width)),
            ),
            scratch_shapes=[pltpu.VMEM((wide, 3 * width), f32)],
        ),
        cost_estimate=pl.CostEstimate(
            flops=12 * rows * wide * width, transcendentals=0, bytes_accessed=16 * rows * wide
        ),
        name="unproject",
    )(places, dq, own, after, before, cosine, sine, act, weight)


def bit_mirror(index, size):
    place = 0
    for b in range(size.bit_length() - 1):
        place = 2 * place + (index // (1 << b)) % 2
    return place


def lay_out_kernel(half, down_rows, up_rows, piece_ref, down_ref, up_ref, out_ref):
    core = pl.program_id(2)
    down_ref[...] = piece_ref[:down_rows].astype(f32)
    out_ref[...] = piece_ref[down_rows + 2 * up_rows :].astype(f32)
    wide = piece_ref.shape[-1]
    for side in range(2):
        rows = slice(down_rows + side * up_rows, down_rows + (side + 1) * up_rows)
        for chunk in range(wide // half):
            slot = side * (wide // half) + chunk
            columns = pl.ds(pl.multiple_of((2 * slot + core) * half, half), half)
            up_ref[:, columns] = piece_ref[rows, chunk * half : (chunk + 1) * half].astype(f32)


def lay_out(everyone, groups, half, down_rows, up_rows, out_rows):
    block, wide = everyone.shape[-2:]
    pairs = 2 * groups

    def kernel(*refs):
        lay_out_kernel(half, down_rows, up_rows, *refs)

    def stacked(h, lo, core):
        return (core * pairs + lo * groups + h, 0)

    return pl.pallas_call(
        kernel,
        out_shape=(
            jax.ShapeDtypeStruct((2 * pairs * down_rows, wide), f32),
            jax.ShapeDtypeStruct((pairs * up_rows, 4 * wide), f32),
            jax.ShapeDtypeStruct((2 * pairs * out_rows, wide), f32),
        ),
        grid=(groups, 2, 2),
        in_specs=[
            pl.BlockSpec((None, block, wide), lambda h, lo, core: (4 * h + 2 * lo + core, 0, 0))
        ],
        out_specs=(
            pl.BlockSpec((down_rows, wide), stacked),
            pl.BlockSpec((up_rows, 4 * wide), lambda h, lo, core: (lo * groups + h, 0)),
            pl.BlockSpec((out_rows, wide), stacked),
        ),
        cost_estimate=pl.CostEstimate(
            flops=0, transcendentals=0, bytes_accessed=6 * everyone.size
        ),
        name="lay_out",
    )(everyone)


def bit_mirror(index, size):
    place = 0
    for b in range(size.bit_length() - 1):
        place = 2 * place + (index // (1 << b)) % 2
    return place


def unfold(pieces, places, groups, rows):
    wide = pieces.shape[-1]
    part, block = wide // QUAD, rows // QUAD

    def kernel(places, *refs):
        out_ref = refs[-1]
        for member in range(QUAD):
            for third in range(3):
                lane = (third * QUAD + member) * part
                for k in range(QUAD):
                    out_ref[k * block : (k + 1) * block, lane : lane + part] = refs[member][
                        third * block : (third + 1) * block, k * part : (k + 1) * part
                    ].astype(f32)

    def source(member):
        turned = 2 * (member % 2) + member // 2
        return lambda group, places: ((turned ^ places[0]) * groups + (group ^ places[1]), 0, 0)

    return pl.pallas_call(
        kernel,
        out_shape=jax.ShapeDtypeStruct((groups * rows, 3 * wide), f32),
        grid_spec=pltpu.PrefetchScalarGridSpec(
            num_scalar_prefetch=1,
            grid=(groups,),
            in_specs=[pl.BlockSpec((None, 3 * block, wide), source(m)) for m in range(QUAD)],
            out_specs=pl.BlockSpec((rows, 3 * wide), lambda group, places: (group, 0)),
        ),
        cost_estimate=pl.CostEstimate(flops=0, transcendentals=0, bytes_accessed=6 * pieces.size),
        name="unfold",
    )(places, *([pieces] * QUAD))


def spread(pieces, places, groups):
    count, rows, wide = pieces.shape
    part = wide // 3

    def kernel(places, *refs):
        out_ref = refs[-1]
        for member in range(QUAD):
            for third in range(3):
                lane = (third * QUAD + member) * part
                out_ref[:, lane : lane + part] = refs[member][
                    :, third * part : (third + 1) * part
                ].astype(f32)

    def source(member):
        turned = 2 * (member % 2) + member // 2
        return lambda group, places: ((turned ^ places[0]) * groups + (group ^ places[1]), 0, 0)

    return pl.pallas_call(
        kernel,
        out_shape=jax.ShapeDtypeStruct((groups * rows, QUAD * wide), f32),
        grid_spec=pltpu.PrefetchScalarGridSpec(
            num_scalar_prefetch=1,
            grid=(groups,),
            in_specs=[pl.BlockSpec((None, rows, wide), source(m)) for m in range(QUAD)],
            out_specs=pl.BlockSpec((rows, QUAD * wide), lambda group, places: (group, 0)),
        ),
        name="spread",
    )(places, *([pieces] * QUAD))


def on_device(
    tokens,
    teacher,
    cotangent,
    doc_starts,
    doc_time,
    valid_mask,
    gain_one,
    bias_one,
    time_one,
    qkv_weight,
    out_weight,
    gain_two,
    bias_two,
    time_two,
    up_weight,
    up_bias,
    down_weight,
    down_bias,
):
    tok_rows = tokens.shape[1]
    width_d = tokens.shape[2]
    shards = lax.axis_size("shard")
    groups = lax.axis_size("hi")
    length = tok_rows * QUAD * groups
    quad_rows = QUAD * tok_rows
    part = LOCAL_HEADS * HEAD
    hi, lo = lax.axis_index("hi"), lax.axis_index("lo")
    core, shard = lax.axis_index("core"), lax.axis_index("shard")
    member = 2 * lo + core
    starts = doc_starts[0]
    slots = starts.shape[0]
    rows_w = qkv_weight.shape[0]

    block_tokens = [tokens[0], flip(tokens[0], "core"), flip(tokens[0], "lo")]
    block_tokens.append(flip(block_tokens[2], "core"))

    def packed(time_weight, vectors):
        rows = [jnp.pad(v.astype(bf16), (0, -v.shape[0] % width_d)) for v in vectors]
        rows = jnp.concatenate(rows).reshape(-1, width_d)
        rows = jnp.pad(rows, ((0, 16 - rows.shape[0]), (0, 0)))
        return jnp.concatenate([time_weight, rows], axis=0)

    def unpacked(gathered):
        blocks = gathered.reshape(shards, -1, width_d)
        return blocks[:, :-16].reshape(TEMB, width_d), blocks[:, -16:]

    own_part = width_d // shards

    def side_by_side(rows):
        return jnp.concatenate([rows[k, :, :own_part] for k in range(shards)], axis=1)

    stamp_high = (doc_time[0] // 8).astype(bf16)
    stamp_low = (doc_time[0] % 8).astype(bf16)
    pack_one = packed(time_one, [gain_one, bias_one, stamp_high, stamp_low])
    pack_two = packed(time_two, [gain_two, bias_two, down_bias, up_bias])
    time_attn, rows_one = unpacked(gather_shard(pack_one))
    vectors_one = side_by_side(rows_one[:, :8]).astype(f32)
    stamps_all = rows_one[:, 2, :slots].astype(f32) * 8.0 + rows_one[:, 3, :slots].astype(f32)

    qkv_part = pick_columns(
        qkv_weight, QUAD * jnp.arange(3, dtype=jnp.int32) + member, part
    )
    if shards == 2:
        qkv_left, qkv_right = qkv_part, flip(qkv_part, "shard")
        qkv_own = in_order(shard, qkv_left, qkv_right, 0)
        left_shard = shard
    else:
        qkv_own = lax.all_gather(qkv_part, "shard", axis=0, tiled=True)
        qkv_left, qkv_right = jnp.split(qkv_own, 2, axis=0)
        left_shard = jnp.zeros_like(shard)

    up_now, down_now, out_now, _ = lax.optimization_barrier(
        (up_weight, down_weight, out_weight, qkv_part)
    )
    time_mlp, rows_two = unpacked(gather_shard(pack_two))
    vectors_two = side_by_side(rows_two[:, :3])
    gain_mlp, bias_mlp, down_bias_full = (vectors_two[k] for k in range(3))
    up_bias_all = rows_two[:, 3:].reshape(shards, -1)[:, : up_bias.shape[0]]
    hidden_half = up_bias.shape[0] // 2
    up_bias_own = lax.dynamic_index_in_dim(
        up_bias_all.reshape(shards, 2, hidden_half), core, 1, keepdims=False
    ).reshape(-1)
    if shards == 2:
        out_part = lax.optimization_barrier((half_of(out_now, core), qkv_right))[0]
        out_own = gather_shard(out_part)
    else:
        out_all = lax.all_gather(out_weight, "shard", axis=0, tiled=True)
        out_own = lax.dynamic_index_in_dim(
            out_all.reshape(2, 2, part, width_d), core, 1, keepdims=False
        ).reshape(2 * part, width_d)
    if shards == 2:
        later = assemble(down_now, up_now, core[None].astype(jnp.int32))
    else:
        up_part = pick_columns(
            up_now, 2 * jnp.arange(shards, dtype=jnp.int32) + core, hidden_half
        )
        later = jnp.concatenate(
            [half_of(down_now, core)]
            + [up_part[:, k * width_d : (k + 1) * width_d] for k in range(2)],
            axis=0,
        )
    vectors_one, later = lax.optimization_barrier((vectors_one, later))
    later = lax.all_gather(later, "shard", axis=0)
    own_rows = later.shape[1] - 2 * rows_w
    down_own = later[:, :own_rows].reshape(-1, width_d)
    up_own = jnp.concatenate(
        [
            later[:, own_rows + k * rows_w : own_rows + (k + 1) * rows_w].reshape(-1, width_d)
            for k in range(2)
        ],
        axis=1,
    )

    block_base = (hi * QUAD + member) * tok_rows
    quad_base = hi * quad_rows
    own_seg = segments_at(starts, block_base + jnp.arange(tok_rows, dtype=jnp.int32))
    one_hot = (own_seg[:, None] == jnp.arange(slots, dtype=jnp.int32)[None, :]).astype(bf16)
    features_all = time_features(stamps_all.reshape(-1)).astype(bf16).reshape(shards, slots, TEMB)
    features_docs = time_features(doc_time[0]).astype(bf16)
    features = times(one_hot, features_docs).astype(bf16)
    quad_places = quad_base + jnp.arange(quad_rows, dtype=jnp.int32)
    quad_begin = begins_at(starts, quad_places)
    quad_end = ends_at(starts, quad_places, length)
    cosine, signed_sine = turn_tables(quad_places - quad_begin)
    reach = jnp.concatenate(
        [
            (quad_begin - quad_base)[None],
            (quad_end - quad_base)[None],
            jnp.zeros((6, quad_rows), jnp.int32),
        ],
        axis=0,
    )

    valid = valid_mask[0].astype(f32)
    counted = jnp.full((8, LANES), jnp.sum(valid))
    counted = sum_all(sum_all(counted, "core", [1]), "lo", [1])

    block_in = tokens[0].astype(f32)
    _, normed_one, scales_one, inv_one = norm_forward(
        block_in, vectors_one[0], vectors_one[1], features, time_attn
    )
    quad_seg = segments_at(starts, quad_places)
    quad_hot = (quad_seg[:, None] == jnp.arange(slots, dtype=jnp.int32)[None, :]).astype(bf16)
    quad_features = times(quad_hot, features_docs).astype(bf16)
    projected = None
    for far in range(2):
        projected = project(
            jnp.stack([member ^ (2 * far), left_shard]).astype(jnp.int32),
            block_tokens[2 * far],
            block_tokens[2 * far + 1],
            quad_features,
            time_attn,
            vectors_one,
            qkv_left,
            qkv_right,
            cosine,
            signed_sine,
            projected,
        )
    act_quad, query_low, kv_pair = projected
    up_pairs = [(i, i + 1) for i in range(groups - 1)]
    down_pairs = [(i + 1, i) for i in range(groups - 1)]
    kv_prev = lax.ppermute(kv_pair, "hi", up_pairs)
    kv_next = lax.ppermute(kv_pair, "hi", down_pairs)

    query_low, counted = lax.optimization_barrier((query_low, counted))

    def ranges(row_shift, row_block, col_shift, col_block):
        return block_ranges(
            starts,
            length,
            quad_base + row_shift,
            row_block,
            quad_base + col_shift,
            col_block,
            quad_rows,
        )

    acc, stat = attend_near(
        ranges(0, BLOCK_Q, 0, BLOCK_K), query_low, kv_pair, reach
    )
    counted = sum_all(counted, "hi", [1])
    counted, acc = lax.optimization_barrier((counted, acc))
    counted = sum_all(counted, "hi", bits_of("hi")[1:])
    mixed_quad, lse = attend_far(
        ranges(0, BLOCK_Q, -quad_rows, BLOCK_K),
        ranges(0, BLOCK_Q, quad_rows, BLOCK_K),
        query_low,
        kv_prev,
        kv_next,
        reach,
        acc,
        stat,
    )

    def to_chip(value):
        kept, sent = half_of(value, lo), half_of(value, 1 - lo)
        return in_order(lo, kept, flip(sent, "lo"), 1)

    def to_quad(value):
        left, right = value[:, :part], value[:, part:]
        kept = jnp.where(lo == 0, left, right)
        sent = jnp.where(lo == 0, right, left)
        return in_order(lo, kept, flip(sent, "lo"), 0)

    def both_cores(value):
        return in_order(core, value, flip(value, "core"), 0)

    def own_tokens(partial):
        sent = flip(half_of(partial, 1 - core).astype(bf16), "core")
        return half_of(partial, core) + sent.astype(f32)

    counted, mixed_quad = lax.optimization_barrier((counted, mixed_quad))
    counted = sum_all(counted, "shard", bits_of("shard"))
    counted, mixed_low = lax.optimization_barrier((counted, to_chip(mixed_quad)))
    counted = counted[0, 0]
    middle = block_in + own_tokens(times(mixed_low, out_own))

    act_pre_two, normed_two, scales_two, inv_two = norm_forward(
        middle, gain_mlp, bias_mlp, features, time_mlp
    )
    act_two = both_cores(act_pre_two.astype(bf16))
    upper_in = times(act_two, up_own) + up_bias_own.astype(f32)[None, :]
    normal_cdf = 0.5 + 0.5 * lax.erf(upper_in * math.sqrt(0.5))
    density = jnp.exp(-0.5 * upper_in * upper_in) * (1.0 / math.sqrt(2.0 * math.pi))
    hidden = (upper_in * normal_cdf).astype(bf16)
    slope = (normal_cdf + upper_in * density).astype(bf16)
    block_out = (
        middle + own_tokens(times(hidden, down_own)) + down_bias_full.astype(f32)[None, :]
    )
    misfit = block_out - teacher[0].astype(f32)
    square_sum = jnp.sum(valid[:, None] * misfit * misfit)
    grad_final = (
        cotangent[0].astype(f32) + 2.0 / (counted * width_d) * valid[:, None] * misfit
    )
    grad_mid_own = grad_final.astype(bf16)
    grad_mid = both_cores(grad_mid_own)
    grad_down_bias = jnp.sum(grad_mid_own.astype(f32), axis=0, keepdims=True)
    grad_upper = (times_trans(grad_mid, down_own) * slope.astype(f32)).astype(bf16)
    grad_up_bias = jnp.sum(grad_upper.astype(f32), axis=0)
    grad_act_two = own_tokens(times_trans(grad_upper, up_own))
    grad_in_two, grad_gain_two, grad_bias_two, by_doc_two = norm_backward(
        grad_act_two, normed_two, scales_two, inv_two, one_hot
    )
    grad_middle = grad_final + grad_in_two
    grad_branch = both_cores(grad_middle.astype(bf16))
    grad_mixed = times_trans(grad_branch, out_own).astype(bf16)
    grad_quad = to_quad(grad_mixed)
    late_upper, late_mid, _ = lax.optimization_barrier((grad_upper, grad_mid, grad_mixed))
    grad_down = contract_rows(hidden, late_mid)
    grad_up = contract_rows(act_two, late_upper)
    grad_out = contract_rows(mixed_low, grad_branch)

    if shards == 2:
        out_rows = grad_out
    else:
        by_core = lax.all_gather(grad_out.astype(bf16), "core", axis=0, tiled=False)
        out_rows = jnp.transpose(
            by_core.reshape(2, 2, part, width_d), (1, 0, 2, 3)
        ).reshape(2 * 2 * part, width_d)
    pairs = 2 * groups
    blocks = [
        grad_down.astype(bf16).reshape(shards, pairs, -1, width_d),
        jnp.concatenate(
            [
                grad_up[:, k * width_d : (k + 1) * width_d]
                .astype(bf16)
                .reshape(shards, pairs, -1, width_d)
                for k in range(2)
            ],
            axis=2,
        ),
        out_rows.astype(bf16).reshape(shards, pairs, -1, width_d),
    ]
    pieces = jnp.concatenate(blocks, axis=2).reshape(-1, width_d)
    pieces = lax.optimization_barrier((pieces, grad_quad))[0]
    reduced = lax.psum_scatter(pieces, ("shard", "lo"), scatter_dimension=0, tiled=True)
    head_of = jnp.arange(part, dtype=jnp.int32) // HEAD
    summing = (jnp.arange(8, dtype=jnp.int32)[:, None] == head_of[None, :]).astype(f32)
    delta = lax.dot_general(
        summing,
        grad_quad.astype(f32) * mixed_quad.astype(f32),
        (((1,), (1,)), ((), ())),
        precision=lax.Precision.HIGHEST,
        preferred_element_type=f32,
    )

    def give_back(row_shift, kv, dq):
        return attend_return(
            row_shift,
            ranges(row_shift, BLOCK_K, 0, BLOCK_Q),
            query_low,
            grad_quad,
            kv,
            reach,
            lse,
            delta,
            dq,
        )

    dq, dkv_prev = give_back(-quad_rows, kv_prev, None)
    from_next = lax.ppermute(dkv_prev, "hi", down_pairs)
    dq, dkv_next = give_back(quad_rows, kv_next, dq)
    from_prev = lax.ppermute(dkv_next, "hi", up_pairs)
    dq, dkv_own = give_back(0, kv_pair, dq)

    act_send, act_keep, qkv_send, qkv_keep = unproject(
        jnp.stack([lo, left_shard]).astype(jnp.int32),
        dq,
        dkv_own,
        from_next,
        from_prev,
        cosine,
        signed_sine,
        act_quad,
        qkv_own,
    )
    act_got = flip(act_send, "lo")
    if shards == 2:
        qkv_rows = qkv_keep + flip(qkv_send, "shard").astype(f32)
    else:
        qkv_rows = jnp.concatenate([qkv_keep, qkv_send.astype(f32)], axis=0)
        qkv_rows = scatter_sum(qkv_rows, "shard", reversed(bits_of("shard")))
    qkv_rows = scatter_sum(qkv_rows, "hi", bits_of("hi")[:1])
    act_got, qkv_rows = lax.optimization_barrier((act_got, qkv_rows))
    grad_act_one = own_tokens(act_keep + act_got.astype(f32))
    grad_in_one, grad_gain_one, grad_bias_one, by_doc_one = norm_backward(
        grad_act_one, normed_one, scales_one, inv_one, one_hot
    )
    input_grad = grad_middle + grad_in_one

    bias_slots = jnp.where(
        jnp.arange(2, dtype=jnp.int32)[None, :, None] == core,
        grad_up_bias.reshape(shards, 1, hidden_half),
        0.0,
    ).reshape(-1, width_d)
    square_top = square_sum.astype(bf16).astype(f32)
    loss_row = jnp.where(jnp.arange(width_d)[None, :] == 0, square_top, square_sum - square_top)
    summed_rows = [grad_gain_one, grad_bias_one, grad_gain_two, grad_bias_two, grad_down_bias]
    small = jnp.concatenate(
        summed_rows + [bias_slots, loss_row, by_doc_one, by_doc_two],
        axis=0,
    )
    filled = small.shape[0]
    small = jnp.pad(small, ((0, -filled % 16), (0, 0)))
    small = small.astype(bf16)
    qkv_rows = scatter_sum(qkv_rows, "hi", bits_of("hi")[1:]).astype(bf16)
    reduced = lax.optimization_barrier((reduced, dkv_own))[0]
    reduced = lax.psum_scatter(reduced, "hi", scatter_dimension=0, tiled=True)
    down_rows, up_rows, out_piece = (b.shape[2] for b in blocks)
    up_rows = up_rows // 2
    if shards == 2:
        part_rows = qkv_rows.shape[0] // QUAD
        turned = [
            jnp.concatenate(
                [
                    qkv_rows[k * part_rows : (k + 1) * part_rows, t * part : (t + 1) * part]
                    for k in range(QUAD)
                ],
                axis=1,
            )
            for t in range(3)
        ]
        reduced = lax.optimization_barrier((reduced, act_got))[0]
        everyone = lax.all_gather(reduced, ("hi", "lo", "core"), axis=0)
        everyone = everyone.reshape(QUAD * groups, -1, width_d)
        rest = jnp.concatenate(turned + [small], axis=0)
        for axis in ("hi", "lo", "core"):
            rest = gather_back(rest, axis)
        everyone, rest = lax.optimization_barrier((everyone, rest))
        rest = rest.reshape(QUAD * groups, -1, width_d)
        small = rest[:, rest.shape[1] - small.shape[0] :]
        down_total, up_total, out_total = lay_out(
            everyone, groups, hidden_half, down_rows, up_rows, out_piece
        )
        places = jnp.stack([2 * core + lo, bit_mirror(hi, groups)]).astype(jnp.int32)
        qkv_total = unfold(rest, places, groups, qkv_rows.shape[0])
    else:
        everyone = lax.all_gather(
            jnp.concatenate([reduced, small], axis=0), ("hi", "lo", "core"), axis=0
        ).reshape(QUAD * groups, -1, width_d)
        filled = everyone.shape[1] - small.shape[0]
        small = everyone[:, filled:]
        everyone = everyone[:, :filled].reshape(pairs, 2, -1, width_d)
        wide = everyone.astype(f32).reshape(groups, 2, 2, -1, width_d)
        wide = jnp.transpose(wide, (1, 0, 2, 3, 4)).reshape(everyone.shape)
        down_total = jnp.transpose(wide[:, :, :down_rows], (1, 0, 2, 3)).reshape(-1, width_d)
        up_piece = wide[:, :, down_rows : down_rows + 2 * up_rows]
        up_piece = up_piece.reshape(pairs, 2, 2, up_rows, shards // 2, hidden_half)
        up_total = jnp.transpose(up_piece, (0, 3, 2, 4, 1, 5)).reshape(rows_w, 4 * width_d)
        out_total = wide[:, 0, down_rows + 2 * up_rows :].reshape(-1, width_d)
        for axis in ("hi", "lo", "core"):
            qkv_rows = gather_back(qkv_rows, axis)
        qkv_total = spread(
            qkv_rows.reshape(QUAD * groups, rows_w // groups, 3 * part),
            jnp.stack([2 * core + lo, bit_mirror(hi, groups)]).astype(jnp.int32),
            groups,
        )

    small = jnp.sum(small.astype(f32), axis=0)
    small_all = gather_shard(small).reshape(shards, -1, width_d)
    bias_rows = bias_slots.shape[0]
    head_rows = 6 + bias_rows
    totals = jnp.sum(small_all[:, :head_rows], axis=0)
    docs_one = small_all[:, head_rows : head_rows + slots]
    docs_two = small_all[:, head_rows + slots : head_rows + 2 * slots]

    def own_vector(row):
        return lax.dynamic_slice_in_dim(row, shard * own_part, own_part, 0)

    own_features = lax.dynamic_slice_in_dim(
        features_all, shard * (TEMB // shards), TEMB // shards, 2
    ).astype(f32)

    def time_total(docs):
        return lax.dot_general(
            own_features,
            docs,
            (((0, 1), (0, 1)), ((), ())),
            precision=lax.Precision.HIGHEST,
            preferred_element_type=f32,
        )

    up_bias_total = lax.dynamic_slice_in_dim(
        totals[5 : 5 + bias_rows].reshape(-1), shard * 2 * hidden_half, 2 * hidden_half, 0
    )
    loss_row = totals[5 + bias_rows]
    loss_value = (loss_row[0] + loss_row[1]) / (counted * width_d)
    return (
        block_out.astype(bf16)[None],
        loss_value,
        input_grad[None],
        own_vector(totals[0]),
        own_vector(totals[1]),
        time_total(docs_one),
        qkv_total,
        out_total,
        own_vector(totals[2]),
        own_vector(totals[3]),
        time_total(docs_two),
        up_total,
        up_bias_total,
        down_total,
        own_vector(totals[4]),
    )


def solution(mesh):
    ctx, shards = mesh.shape["ctx"], mesh.shape["shard"]
    fine = Mesh(
        mesh.devices.reshape(ctx // QUAD, 2, 2, shards), ("hi", "lo", "core", "shard")
    )
    blocks = ("hi", "lo", "core")
    in_specs = (
        P("shard", blocks, None),
        P("shard", blocks, None),
        P("shard", blocks, None),
        P("shard", None),
        P("shard", None),
        P("shard", blocks),
        P("shard"),
        P("shard"),
        P("shard", None),
        P("shard", None),
        P("shard", None),
        P("shard"),
        P("shard"),
        P("shard", None),
        P("shard", None),
        P("shard"),
        P("shard", None),
        P("shard"),
    )
    out_specs = (
        P("shard", blocks, None),
        P(),
        P("shard", blocks, None),
        P("shard"),
        P("shard"),
        P("shard", None),
        P("shard", None),
        P("shard", None),
        P("shard"),
        P("shard"),
        P("shard", None),
        P("shard", None),
        P("shard"),
        P("shard", None),
        P("shard"),
    )
    return jax.shard_map(
        on_device, mesh=fine, in_specs=in_specs, out_specs=out_specs, check_vma=False
    )
```

```python
import math

import jax
import jax.numpy as jnp
from jax import lax
from jax.experimental import pallas as pl
from jax.experimental.pallas import tpu as pltpu
from jax.sharding import Mesh
from jax.sharding import PartitionSpec as P

HEADS = 16
HEAD = 64
TEMB = 256
QUAD = 4
LOCAL_HEADS = HEADS // QUAD
LANES = 128
BLOCK_Q = 512
BLOCK_K = 512
norm_eps = 1e-05
masked_value = -1e30
LOG2E = math.log2(math.e)
bf16 = jnp.bfloat16
f32 = jnp.float32


def flip(value, axis):
    return lax.ppermute(value, axis, [(0, 1), (1, 0)])


def in_order(index, own, other, axis):
    return jnp.where(
        index == 0,
        jnp.concatenate([own, other], axis=axis),
        jnp.concatenate([other, own], axis=axis),
    )


def half_of(value, index):
    rows = value.shape[0] // 2
    return lax.dynamic_slice_in_dim(value, index * rows, rows, 0)


def xor_pairs(size, bit):
    return [(i, i ^ bit) for i in range(size)]


def bits_of(axis):
    return [1 << b for b in range(lax.axis_size(axis).bit_length() - 1)]


def scatter_sum(value, axis, bits):
    size = lax.axis_size(axis)
    for bit in bits:
        mine = (lax.axis_index(axis) // bit) % 2
        sent = half_of(value, 1 - mine).astype(bf16)
        got = lax.ppermute(sent, axis, xor_pairs(size, bit))
        value = half_of(value, mine).astype(f32) + got.astype(f32)
    return value


def gather_back(value, axis):
    size = lax.axis_size(axis)
    for bit in reversed(bits_of(axis)):
        got = lax.ppermute(value, axis, xor_pairs(size, bit))
        value = jnp.concatenate([value, got], axis=0)
    return value


def sum_all(value, axis, bits):
    size = lax.axis_size(axis)
    for bit in bits:
        value = value + lax.ppermute(value, axis, xor_pairs(size, bit))
    return value


def gather_shard(value):
    if lax.axis_size("shard") == 2:
        return in_order(lax.axis_index("shard"), value, flip(value, "shard"), 0)
    return lax.all_gather(value, "shard", axis=0, tiled=True)


def contract_rows(left_side, right_side):
    return lax.dot_general(
        left_side, right_side, (((0,), (0,)), ((), ())), preferred_element_type=f32
    )


def times_trans(left_side, right_side):
    return lax.dot_general(
        left_side, right_side, (((1,), (1,)), ((), ())), preferred_element_type=f32
    )


def times(left_side, right_side):
    return jnp.dot(left_side, right_side, preferred_element_type=f32)


def segments_at(starts, places):
    return jnp.sum((starts[None, :] <= places[:, None]).astype(jnp.int32), axis=1) - 1


def begins_at(starts, places):
    return jnp.max(jnp.where(starts[None, :] <= places[:, None], starts[None, :], 0), axis=1)


def ends_at(starts, places, length):
    return jnp.min(jnp.where(starts[None, :] > places[:, None], starts[None, :], length), axis=1)


def block_ranges(starts, length, row_base, row_block, col_base, col_block, tokens):
    count = tokens // row_block
    first = row_base + row_block * jnp.arange(count, dtype=jnp.int32)
    last = first + row_block - 1
    real = jnp.logical_and(first >= 0, last < length)
    low = jnp.clip(begins_at(starts, first) - col_base, 0, tokens)
    high = jnp.clip(ends_at(starts, last, length) - col_base, 0, tokens)
    live = jnp.logical_and(real, high > low)
    low = low // LANES * LANES
    blocks = jnp.where(live, (high - low + col_block - 1) // col_block, 0)
    low = jnp.minimum(low, tokens - blocks * col_block)
    return jnp.stack([low, blocks]).astype(jnp.int32)


def time_features(time_index):
    halfway = TEMB // 2
    ladder = jnp.exp(-math.log(10000.0) * jnp.arange(halfway, dtype=f32) / halfway)
    phases = time_index.astype(f32)[:, None] * ladder[None, :]
    return jnp.concatenate([jnp.sin(phases), jnp.cos(phases)], axis=1)


def turn_tables(places):
    halfway = HEAD // 2
    ladder = jnp.exp(-math.log(10000.0) * 2.0 * jnp.arange(halfway, dtype=f32) / HEAD)
    turned = places.astype(f32)[:, None] * jnp.tile(ladder, LANES // halfway)[None, :]
    sign = jnp.where(jnp.arange(LANES) % HEAD < halfway, -1.0, 1.0).astype(f32)
    return jnp.cos(turned), jnp.sin(turned) * sign[None, :]


def norm_forward(values, gain_vec, bias_vec, features, time_weight):
    average = jnp.mean(values, axis=1, keepdims=True)
    centred = values - average
    inv_std = lax.rsqrt(jnp.mean(centred * centred, axis=1, keepdims=True) + norm_eps)
    normed = centred * inv_std
    scales = gain_vec.astype(f32)[None, :] + times(features, time_weight)
    return (normed * scales + bias_vec.astype(f32)[None, :], normed, scales, inv_std)


def norm_backward(grad_act, normed, scales, inv_std, one_hot):
    grad_scale = grad_act * normed
    grad_gain = jnp.sum(grad_scale, axis=0, keepdims=True)
    grad_bias = jnp.sum(grad_act, axis=0, keepdims=True)
    by_doc = contract_rows(one_hot, grad_scale.astype(bf16))
    grad_norm = grad_act * scales
    grad_input = inv_std * (
        grad_norm
        - jnp.mean(grad_norm, axis=1, keepdims=True)
        - normed * jnp.mean(grad_norm * normed, axis=1, keepdims=True)
    )
    return (grad_input, grad_gain, grad_bias, by_doc)


def pick_kernel(picks, weight_ref, out_ref):
    out_ref[...] = weight_ref[...]


def pick_columns(weight, picks, block):
    rows, count = weight.shape[0], picks.shape[0]
    return pl.pallas_call(
        pick_kernel,
        out_shape=jax.ShapeDtypeStruct((rows, count * block), weight.dtype),
        grid_spec=pltpu.PrefetchScalarGridSpec(
            num_scalar_prefetch=1,
            grid=(count,),
            in_specs=[pl.BlockSpec((rows, block), lambda i, p: (0, p[i]))],
            out_specs=pl.BlockSpec((rows, block), lambda i, p: (0, i)),
        ),
        cost_estimate=pl.CostEstimate(
            flops=0, transcendentals=0, bytes_accessed=4 * rows * count * block
        ),
        name="pick_columns",
    )(picks, weight)


def assemble_kernel(core, down_ref, up_ref, out_ref):
    early = pl.program_id(0) < pl.num_programs(0) // 2
    out_ref[...] = jnp.where(early, down_ref[...], up_ref[...])


def assemble(down, up, core):
    wide, rows = down.shape[1], up.shape[0]
    count = down.shape[0] // 2 // rows
    return pl.pallas_call(
        assemble_kernel,
        out_shape=jax.ShapeDtypeStruct((2 * count * rows, wide), down.dtype),
        grid_spec=pltpu.PrefetchScalarGridSpec(
            num_scalar_prefetch=1,
            grid=(2 * count,),
            in_specs=[
                pl.BlockSpec(
                    (rows, wide), lambda i, core: (core[0] * count + jnp.minimum(i, count - 1), 0)
                ),
                pl.BlockSpec(
                    (rows, wide), lambda i, core: (0, 2 * jnp.maximum(i - count, 0) + core[0])
                ),
            ],
            out_specs=pl.BlockSpec((rows, wide), lambda i, core: (i, 0)),
        ),
        cost_estimate=pl.CostEstimate(
            flops=0, transcendentals=0, bytes_accessed=6 * down.size
        ),
        name="assemble",
    )(core, down, up)


def lane_halves(value):
    lane = lax.broadcasted_iota(jnp.int32, value.shape, 1)
    zero = jnp.zeros_like(value)
    return jnp.where(lane < HEAD, value, zero), jnp.where(lane < HEAD, zero, value)


def within(reach, first, side):
    begins, ends = reach
    place = lax.broadcasted_iota(jnp.int32, (BLOCK_K, BLOCK_Q), 0)
    if side < 0:
        return place >= begins - first
    if side > 0:
        return place < ends - first
    return jnp.logical_and(place >= begins - first, place < ends - first)


def pair_lanes(pair, base=0):
    return pl.ds(pl.multiple_of(base + pair * LANES, LANES), LANES)


def look_through(bounds, step, queries, kv_ref, pair, reach, base, where, state):
    def visit(block, carried):
        first = pl.multiple_of(bounds[0, step] + block * BLOCK_K, LANES)
        rows = pl.ds(first, BLOCK_K)
        keys = kv_ref[rows, pair_lanes(pair)]
        values = kv_ref[rows, pair_lanes(pair, LOCAL_HEADS * HEAD)]
        allowed = within(reach, base + first, where)
        after = []
        for side in range(2):
            top_old, total_old, acc_old = carried[side]
            scores = jnp.where(allowed, times_trans(keys, queries[side]), masked_value)
            top = jnp.maximum(top_old, jnp.max(scores, axis=0, keepdims=True))
            weights = jnp.exp2(scores - top)
            scale = jnp.exp2(top_old - top)
            total = total_old * scale + jnp.sum(weights, axis=0, keepdims=True)
            acc = acc_old * scale + contract_rows(
                values[:, side * HEAD : (side + 1) * HEAD], weights.astype(bf16)
            )
            after.append((top, total, acc))
        return tuple(after)

    return lax.fori_loop(0, bounds[1, step], visit, state)


def near_kernel(bounds, query_ref, kv_ref, reach_ref, acc_ref, stat_ref):
    step = pl.program_id(0)
    reach = (reach_ref[0:1, :], reach_ref[1:2, :])

    @pl.loop(0, LOCAL_HEADS // 2)
    def _(pair):
        queries = lane_halves(query_ref[:, pair_lanes(pair)])
        top = jnp.full((1, BLOCK_Q), masked_value, f32)
        total = jnp.zeros((1, BLOCK_Q), f32)
        acc = jnp.zeros((HEAD, BLOCK_Q), f32)
        state = ((top, total, acc), (top, total, acc))
        state = look_through(bounds, step, queries, kv_ref, pair, reach, 0, 0, state)
        for side in range(2):
            head = 2 * pair + side
            stat_ref[pl.ds(head, 1), :] = state[side][0]
            stat_ref[pl.ds(LOCAL_HEADS + head, 1), :] = state[side][1]
            acc_ref[pl.ds(pl.multiple_of(head * HEAD, HEAD), HEAD), :] = state[side][2]


def far_kernel(
    before,
    after,
    query_ref,
    prev_ref,
    next_ref,
    reach_ref,
    acc_in,
    stat_in,
    out_ref,
    lse_ref,
):
    step = pl.program_id(0)
    tokens = prev_ref.shape[0]
    reach = (reach_ref[0:1, :], reach_ref[1:2, :])
    lse_ref[...] = jnp.zeros_like(lse_ref)

    @pl.loop(0, LOCAL_HEADS // 2)
    def _(pair):
        queries = lane_halves(query_ref[:, pair_lanes(pair)])
        state = tuple(
            (
                stat_in[pl.ds(head, 1), :],
                stat_in[pl.ds(LOCAL_HEADS + head, 1), :],
                acc_in[pl.ds(pl.multiple_of(head * HEAD, HEAD), HEAD), :],
            )
            for head in (2 * pair, 2 * pair + 1)
        )
        state = look_through(before, step, queries, prev_ref, pair, reach, -tokens, -1, state)
        state = look_through(after, step, queries, next_ref, pair, reach, tokens, 1, state)
        mixed = []
        for side in range(2):
            top, total, acc = state[side]
            lse_ref[pl.ds(2 * pair + side, 1), :] = top + jnp.log2(total)
            mixed.append(acc / total)
        out_ref[:, pair_lanes(pair)] = jnp.transpose(jnp.concatenate(mixed, axis=0)).astype(
            out_ref.dtype
        )


def whole(shape):
    return pl.BlockSpec(shape, lambda i, *_: (0,) * len(shape))


def guess(tokens, width, matmuls):
    work = 2 * tokens * (tokens // 2) * width * matmuls * 3
    return pl.CostEstimate(
        flops=work, transcendentals=tokens * tokens * LOCAL_HEADS // 2, bytes_accessed=8 * tokens * width
    )


def attend_near(bounds, query, kv_pair, reach):
    tokens, width = query.shape
    return pl.pallas_call(
        near_kernel,
        out_shape=(
            jax.ShapeDtypeStruct((width, tokens), f32),
            jax.ShapeDtypeStruct((8, tokens), f32),
        ),
        grid_spec=pltpu.PrefetchScalarGridSpec(
            num_scalar_prefetch=1,
            grid=(tokens // BLOCK_Q,),
            in_specs=[
                pl.BlockSpec((BLOCK_Q, width), lambda i, b: (i, 0)),
                whole((tokens, 2 * width)),
                pl.BlockSpec((8, BLOCK_Q), lambda i, b: (0, i)),
            ],
            out_specs=(
                pl.BlockSpec((width, BLOCK_Q), lambda i, b: (0, i)),
                pl.BlockSpec((8, BLOCK_Q), lambda i, b: (0, i)),
            ),
        ),
        cost_estimate=guess(tokens, width, 4),
        name="attend_near",
    )(bounds, query, kv_pair, reach)


def attend_far(before, after, query, kv_prev, kv_next, reach, acc, stat):
    tokens, width = query.shape
    return pl.pallas_call(
        far_kernel,
        out_shape=(
            jax.ShapeDtypeStruct((tokens, width), bf16),
            jax.ShapeDtypeStruct((8, tokens), f32),
        ),
        grid_spec=pltpu.PrefetchScalarGridSpec(
            num_scalar_prefetch=2,
            grid=(tokens // BLOCK_Q,),
            in_specs=[
                pl.BlockSpec((BLOCK_Q, width), lambda i, b, a: (i, 0)),
                whole((tokens, 2 * width)),
                whole((tokens, 2 * width)),
                pl.BlockSpec((8, BLOCK_Q), lambda i, b, a: (0, i)),
                pl.BlockSpec((width, BLOCK_Q), lambda i, b, a: (0, i)),
                pl.BlockSpec((8, BLOCK_Q), lambda i, b, a: (0, i)),
            ],
            out_specs=(
                pl.BlockSpec((BLOCK_Q, width), lambda i, b, a: (i, 0)),
                pl.BlockSpec((8, BLOCK_Q), lambda i, b, a: (0, i)),
            ),
        ),
        cost_estimate=guess(tokens, width, 2),
        name="attend_far",
    )(before, after, query, kv_prev, kv_next, reach, acc, stat)


def return_kernel(first, shift, bounds, query_ref, grad_ref, kv_ref, reach_ref, lse_ref, delta_ref, *refs):
    dq_ref, dkv_ref = refs[-2:]
    step = pl.program_id(0)
    width = LOCAL_HEADS * HEAD

    @pl.when(step == 0)
    def _():
        dq_ref[...] = jnp.zeros_like(dq_ref) if first else refs[0][...]

    reach_base = shift + step * BLOCK_K

    @pl.loop(0, LOCAL_HEADS // 2)
    def _(pair):
        lanes = pair_lanes(pair)
        keys = lane_halves(kv_ref[:, lanes])
        values = lane_halves(kv_ref[:, pair_lanes(pair, width)])
        keys_t = jnp.transpose(kv_ref[:, lanes].astype(f32)).astype(bf16)

        def visit(block, carried):
            dk, dv = carried
            rows = pl.ds(pl.multiple_of(bounds[0, step] + block * BLOCK_Q, LANES), BLOCK_Q)
            query_pair = query_ref[rows, lanes]
            grad_pair = grad_ref[rows, lanes]
            queries = lane_halves(query_pair)
            grads = lane_halves(grad_pair)
            reach = (reach_ref[0:1, rows], reach_ref[1:2, rows])
            allowed = within(reach, reach_base, shift)
            for side in range(2):
                head = 2 * pair + side
                scores = times_trans(keys[side], query_pair) - lse_ref[pl.ds(head, 1), rows]
                prob = jnp.exp2(jnp.where(allowed, scores, masked_value))
                grad_prob = times_trans(values[side], grad_pair) - delta_ref[pl.ds(head, 1), rows]
                grad_scores = (prob * grad_prob).astype(bf16)
                dv = dv + times(prob.astype(bf16), grads[side])
                dk = dk + times(grad_scores, queries[side])
                head_rows = pl.ds(pl.multiple_of(head * HEAD, HEAD), HEAD)
                dq_ref[head_rows, rows] += times(
                    keys_t[side * HEAD : (side + 1) * HEAD], grad_scores
                )
            return dk, dv

        start = jnp.zeros((BLOCK_K, LANES), f32)
        dk, dv = lax.fori_loop(0, bounds[1, step], visit, (start, start))
        dkv_ref[:, lanes] = (dk * (1.0 / LOG2E)).astype(dkv_ref.dtype)
        dkv_ref[:, pair_lanes(pair, width)] = dv.astype(dkv_ref.dtype)


def attend_return(shift, bounds, query, grad, kv_pair, reach, lse, delta, dq):
    tokens, width = query.shape
    first = dq is None
    specs = [
        whole((tokens, width)),
        whole((tokens, width)),
        pl.BlockSpec((BLOCK_K, 2 * width), lambda i, b: (i, 0)),
        whole((8, tokens)),
        whole((8, tokens)),
        whole((8, tokens)),
    ]
    operands = [bounds, query, grad, kv_pair, reach, lse, delta]
    if not first:
        specs.append(whole((width, tokens)))
        operands.append(dq)

    def kernel(*refs):
        return_kernel(first, shift, *refs)

    return pl.pallas_call(
        kernel,
        out_shape=(
            jax.ShapeDtypeStruct((width, tokens), f32),
            jax.ShapeDtypeStruct((tokens, 2 * width), bf16),
        ),
        grid_spec=pltpu.PrefetchScalarGridSpec(
            num_scalar_prefetch=1,
            grid=(tokens // BLOCK_K,),
            in_specs=specs,
            out_specs=(
                whole((width, tokens)),
                pl.BlockSpec((BLOCK_K, 2 * width), lambda i, b: (i, 0)),
            ),
        ),
        cost_estimate=guess(tokens, width, 5),
        name="attend_return",
    )(*operands)


def project_kernel(
    places,
    own_ref,
    other_ref,
    feature_ref,
    time_ref,
    vector_ref,
    left_ref,
    right_ref,
    cosine_ref,
    sine_ref,
    *refs,
):
    act_ref, query_ref, kv_ref = refs[-3:]
    width = query_ref.shape[1]
    early = pl.program_id(0) < pl.num_programs(0) // 2
    values = jnp.where(early, own_ref[...], other_ref[...]).astype(f32)
    average = jnp.mean(values, axis=1, keepdims=True)
    centred = values - average
    inv_std = lax.rsqrt(jnp.mean(centred * centred, axis=1, keepdims=True) + norm_eps)
    scales = vector_ref[0:1, :] + times(feature_ref[...], time_ref[...])
    act_ref[...] = (centred * inv_std * scales + vector_ref[1:2, :]).astype(bf16)
    half = left_ref.shape[0]
    first = pl.multiple_of(places[1] * half, half)
    second = pl.multiple_of((1 - places[1]) * half, half)
    joined = times(act_ref[:, pl.ds(first, half)], left_ref[...]) + times(
        act_ref[:, pl.ds(second, half)], right_ref[...]
    )
    cosine = jnp.concatenate([cosine_ref[...]] * (width // LANES), axis=1)
    sine = jnp.concatenate([sine_ref[...]] * (width // LANES), axis=1)
    query = turn_lanes(joined[:, :width], cosine, sine)
    query_ref[...] = (query * (LOG2E * HEAD**-0.5)).astype(bf16)
    kv_ref[:, :width] = turn_lanes(joined[:, width : 2 * width], cosine, sine).astype(bf16)
    kv_ref[:, width:] = joined[:, 2 * width :].astype(bf16)


def turn_lanes(vectors, cosine, signed_sine):
    halfway = HEAD // 2
    lane = lax.broadcasted_iota(jnp.int32, vectors.shape, 1) % HEAD
    from_right = pltpu.roll(vectors, vectors.shape[1] - halfway, 1)
    from_left = pltpu.roll(vectors, halfway, 1)
    return vectors * cosine + jnp.where(lane < halfway, from_right, from_left) * signed_sine


def project(places, own, other, features, time_full, vectors, left, right, cosine, sine, before):
    rows, wide = own.shape
    width = left.shape[1] // 3
    step = min(rows, 256)
    count = rows // step

    def placed(columns):
        return pl.BlockSpec(
            (step, columns),
            lambda i, places: ((places[0] ^ (i // count)) * count + i % count, 0),
        )

    in_specs = [
        pl.BlockSpec((step, wide), lambda i, places: (jnp.minimum(i, count - 1), 0)),
        pl.BlockSpec((step, wide), lambda i, places: (jnp.maximum(i - count, 0), 0)),
        placed(TEMB),
        whole(time_full.shape),
        whole(vectors.shape),
        whole(left.shape),
        whole(right.shape),
        placed(LANES),
        placed(LANES),
    ]
    operands = [own, other, features, time_full, vectors, left, right, cosine, sine]
    aliases = {}
    if before is not None:
        for k, array in enumerate(before):
            aliases[1 + len(operands)] = k
            operands.append(array)
            in_specs.append(pl.BlockSpec(memory_space=pl.ANY))
    return pl.pallas_call(
        project_kernel,
        out_shape=(
            jax.ShapeDtypeStruct((QUAD * rows, wide), bf16),
            jax.ShapeDtypeStruct((QUAD * rows, width), bf16),
            jax.ShapeDtypeStruct((QUAD * rows, 2 * width), bf16),
        ),
        grid_spec=pltpu.PrefetchScalarGridSpec(
            num_scalar_prefetch=1,
            grid=(2 * count,),
            in_specs=in_specs,
            out_specs=(placed(wide), placed(width), placed(2 * width)),
        ),
        input_output_aliases=aliases,
        cost_estimate=pl.CostEstimate(
            flops=4 * rows * wide * 4 * width, transcendentals=0, bytes_accessed=16 * rows * wide
        ),
        name="project",
    )(places, *operands)


def unproject_kernel(
    places,
    dq_ref,
    own_ref,
    next_ref,
    prev_ref,
    cosine_ref,
    sine_ref,
    act_ref,
    weight_ref,
    send_ref,
    keep_ref,
    grad_send_ref,
    grad_keep_ref,
    grad_acc,
):
    step, steps = pl.program_id(0), pl.num_programs(0)
    width = dq_ref.shape[0]
    cosine = jnp.concatenate([cosine_ref[...]] * (width // LANES), axis=1)
    sine = jnp.concatenate([sine_ref[...]] * (width // LANES), axis=1)
    dkv = own_ref[...].astype(f32) + next_ref[...].astype(f32) + prev_ref[...].astype(f32)
    dq = jnp.transpose(dq_ref[...]) * HEAD**-0.5
    grad_joined = jnp.concatenate(
        [
            turn_lanes(dq, cosine, -sine).astype(bf16),
            turn_lanes(dkv[:, :width], cosine, -sine).astype(bf16),
            dkv[:, width:].astype(bf16),
        ],
        axis=1,
    )
    partial_act = times_trans(grad_joined, weight_ref[...])

    @pl.when(step < steps // 2)
    def _():
        send_ref[...] = partial_act.astype(bf16)

    @pl.when(step >= steps // 2)
    def _():
        keep_ref[...] = partial_act

    grad = contract_rows(act_ref[...], grad_joined)

    @pl.when(step == 0)
    def _():
        grad_acc[...] = grad

    @pl.when(step > 0)
    def _():
        grad_acc[...] += grad

    @pl.when(step == steps - 1)
    def _():
        half = grad_acc.shape[0] // 2
        sent = pl.multiple_of((1 - places[1]) * half, half)
        kept = pl.multiple_of(places[1] * half, half)
        grad_send_ref[...] = grad_acc[pl.ds(sent, half), :].astype(bf16)
        grad_keep_ref[...] = grad_acc[pl.ds(kept, half), :]


def unproject(places, dq, own, after, before, cosine, sine, act, weight):
    width, rows = dq.shape
    wide = act.shape[1]
    steps = 4
    step = rows // steps

    def order(i, places):
        return (i + (1 - places[0]) * (steps // 2)) % steps

    def rowed(columns):
        return pl.BlockSpec((step, columns), lambda i, places: (order(i, places), 0))

    return pl.pallas_call(
        unproject_kernel,
        out_shape=(
            jax.ShapeDtypeStruct((rows // 2, wide), bf16),
            jax.ShapeDtypeStruct((rows // 2, wide), f32),
            jax.ShapeDtypeStruct((wide // 2, 3 * width), bf16),
            jax.ShapeDtypeStruct((wide // 2, 3 * width), f32),
        ),
        grid_spec=pltpu.PrefetchScalarGridSpec(
            num_scalar_prefetch=1,
            grid=(steps,),
            in_specs=[
                pl.BlockSpec((width, step), lambda i, places: (0, order(i, places))),
                rowed(2 * width),
                rowed(2 * width),
                rowed(2 * width),
                rowed(LANES),
                rowed(LANES),
                rowed(wide),
                whole(weight.shape),
            ],
            out_specs=(
                pl.BlockSpec((step, wide), lambda i, places: (jnp.minimum(i, steps // 2 - 1), 0)),
                pl.BlockSpec((step, wide), lambda i, places: (jnp.maximum(i - steps // 2, 0), 0)),
                whole((wide // 2, 3 * width)),
                whole((wide // 2, 3 * width)),
            ),
            scratch_shapes=[pltpu.VMEM((wide, 3 * width), f32)],
        ),
        cost_estimate=pl.CostEstimate(
            flops=12 * rows * wide * width, transcendentals=0, bytes_accessed=16 * rows * wide
        ),
        name="unproject",
    )(places, dq, own, after, before, cosine, sine, act, weight)


def bit_mirror(index, size):
    place = 0
    for b in range(size.bit_length() - 1):
        place = 2 * place + (index // (1 << b)) % 2
    return place


def lay_out_kernel(half, down_rows, up_rows, piece_ref, down_ref, up_ref, out_ref):
    core = pl.program_id(2)
    down_ref[...] = piece_ref[:down_rows].astype(f32)
    out_ref[...] = piece_ref[down_rows + 2 * up_rows :].astype(f32)
    wide = piece_ref.shape[-1]
    for side in range(2):
        rows = slice(down_rows + side * up_rows, down_rows + (side + 1) * up_rows)
        for chunk in range(wide // half):
            slot = side * (wide // half) + chunk
            columns = pl.ds(pl.multiple_of((2 * slot + core) * half, half), half)
            up_ref[:, columns] = piece_ref[rows, chunk * half : (chunk + 1) * half].astype(f32)


def lay_out(everyone, groups, half, down_rows, up_rows, out_rows):
    block, wide = everyone.shape[-2:]
    pairs = 2 * groups

    def kernel(*refs):
        lay_out_kernel(half, down_rows, up_rows, *refs)

    def stacked(h, lo, core):
        return (core * pairs + lo * groups + h, 0)

    return pl.pallas_call(
        kernel,
        out_shape=(
            jax.ShapeDtypeStruct((2 * pairs * down_rows, wide), f32),
            jax.ShapeDtypeStruct((pairs * up_rows, 4 * wide), f32),
            jax.ShapeDtypeStruct((2 * pairs * out_rows, wide), f32),
        ),
        grid=(groups, 2, 2),
        in_specs=[
            pl.BlockSpec((None, block, wide), lambda h, lo, core: (4 * h + 2 * lo + core, 0, 0))
        ],
        out_specs=(
            pl.BlockSpec((down_rows, wide), stacked),
            pl.BlockSpec((up_rows, 4 * wide), lambda h, lo, core: (lo * groups + h, 0)),
            pl.BlockSpec((out_rows, wide), stacked),
        ),
        cost_estimate=pl.CostEstimate(
            flops=0, transcendentals=0, bytes_accessed=6 * everyone.size
        ),
        name="lay_out",
    )(everyone)


def bit_mirror(index, size):
    place = 0
    for b in range(size.bit_length() - 1):
        place = 2 * place + (index // (1 << b)) % 2
    return place


def unfold(pieces, places, groups, rows):
    wide = pieces.shape[-1]
    part, block = wide // QUAD, rows // QUAD

    def kernel(places, *refs):
        out_ref = refs[-1]
        for member in range(QUAD):
            for third in range(3):
                lane = (third * QUAD + member) * part
                for k in range(QUAD):
                    out_ref[k * block : (k + 1) * block, lane : lane + part] = refs[member][
                        third * block : (third + 1) * block, k * part : (k + 1) * part
                    ].astype(f32)

    def source(member):
        turned = 2 * (member % 2) + member // 2
        return lambda group, places: ((turned ^ places[0]) * groups + (group ^ places[1]), 0, 0)

    return pl.pallas_call(
        kernel,
        out_shape=jax.ShapeDtypeStruct((groups * rows, 3 * wide), f32),
        grid_spec=pltpu.PrefetchScalarGridSpec(
            num_scalar_prefetch=1,
            grid=(groups,),
            in_specs=[pl.BlockSpec((None, 3 * block, wide), source(m)) for m in range(QUAD)],
            out_specs=pl.BlockSpec((rows, 3 * wide), lambda group, places: (group, 0)),
        ),
        cost_estimate=pl.CostEstimate(flops=0, transcendentals=0, bytes_accessed=6 * pieces.size),
        name="unfold",
    )(places, *([pieces] * QUAD))


def spread(pieces, places, groups):
    count, rows, wide = pieces.shape
    part = wide // 3

    def kernel(places, *refs):
        out_ref = refs[-1]
        for member in range(QUAD):
            for third in range(3):
                lane = (third * QUAD + member) * part
                out_ref[:, lane : lane + part] = refs[member][
                    :, third * part : (third + 1) * part
                ].astype(f32)

    def source(member):
        turned = 2 * (member % 2) + member // 2
        return lambda group, places: ((turned ^ places[0]) * groups + (group ^ places[1]), 0, 0)

    return pl.pallas_call(
        kernel,
        out_shape=jax.ShapeDtypeStruct((groups * rows, QUAD * wide), f32),
        grid_spec=pltpu.PrefetchScalarGridSpec(
            num_scalar_prefetch=1,
            grid=(groups,),
            in_specs=[pl.BlockSpec((None, rows, wide), source(m)) for m in range(QUAD)],
            out_specs=pl.BlockSpec((rows, QUAD * wide), lambda group, places: (group, 0)),
        ),
        name="spread",
    )(places, *([pieces] * QUAD))


def on_device(
    tokens,
    teacher,
    cotangent,
    doc_starts,
    doc_time,
    valid_mask,
    gain_one,
    bias_one,
    time_one,
    qkv_weight,
    out_weight,
    gain_two,
    bias_two,
    time_two,
    up_weight,
    up_bias,
    down_weight,
    down_bias,
):
    tok_rows = tokens.shape[1]
    width_d = tokens.shape[2]
    shards = lax.axis_size("shard")
    groups = lax.axis_size("hi")
    length = tok_rows * QUAD * groups
    quad_rows = QUAD * tok_rows
    part = LOCAL_HEADS * HEAD
    hi, lo = lax.axis_index("hi"), lax.axis_index("lo")
    core, shard = lax.axis_index("core"), lax.axis_index("shard")
    member = 2 * lo + core
    starts = doc_starts[0]
    slots = starts.shape[0]
    rows_w = qkv_weight.shape[0]

    block_tokens = [tokens[0], flip(tokens[0], "core"), flip(tokens[0], "lo")]
    block_tokens.append(flip(block_tokens[2], "core"))

    def packed(time_weight, vectors):
        rows = [jnp.pad(v.astype(bf16), (0, -v.shape[0] % width_d)) for v in vectors]
        rows = jnp.concatenate(rows).reshape(-1, width_d)
        rows = jnp.pad(rows, ((0, 16 - rows.shape[0]), (0, 0)))
        return jnp.concatenate([time_weight, rows], axis=0)

    def unpacked(gathered):
        blocks = gathered.reshape(shards, -1, width_d)
        return blocks[:, :-16].reshape(TEMB, width_d), blocks[:, -16:]

    own_part = width_d // shards

    def side_by_side(rows):
        return jnp.concatenate([rows[k, :, :own_part] for k in range(shards)], axis=1)

    stamp_high = (doc_time[0] // 8).astype(bf16)
    stamp_low = (doc_time[0] % 8).astype(bf16)
    pack_one = packed(time_one, [gain_one, bias_one, stamp_high, stamp_low])
    pack_two = packed(time_two, [gain_two, bias_two, down_bias, up_bias])
    time_attn, rows_one = unpacked(gather_shard(pack_one))
    vectors_one = side_by_side(rows_one[:, :8]).astype(f32)
    stamps_all = rows_one[:, 2, :slots].astype(f32) * 8.0 + rows_one[:, 3, :slots].astype(f32)

    qkv_part = pick_columns(
        qkv_weight, QUAD * jnp.arange(3, dtype=jnp.int32) + member, part
    )
    if shards == 2:
        qkv_left, qkv_right = qkv_part, flip(qkv_part, "shard")
        qkv_own = in_order(shard, qkv_left, qkv_right, 0)
        left_shard = shard
    else:
        qkv_own = lax.all_gather(qkv_part, "shard", axis=0, tiled=True)
        qkv_left, qkv_right = jnp.split(qkv_own, 2, axis=0)
        left_shard = jnp.zeros_like(shard)

    up_now, down_now, out_now, _ = lax.optimization_barrier(
        (up_weight, down_weight, out_weight, qkv_part)
    )
    time_mlp, rows_two = unpacked(gather_shard(pack_two))
    vectors_two = side_by_side(rows_two[:, :3])
    gain_mlp, bias_mlp, down_bias_full = (vectors_two[k] for k in range(3))
    up_bias_all = rows_two[:, 3:].reshape(shards, -1)[:, : up_bias.shape[0]]
    hidden_half = up_bias.shape[0] // 2
    up_bias_own = lax.dynamic_index_in_dim(
        up_bias_all.reshape(shards, 2, hidden_half), core, 1, keepdims=False
    ).reshape(-1)
    if shards == 2:
        out_part = lax.optimization_barrier((half_of(out_now, core), qkv_right))[0]
        out_own = gather_shard(out_part)
    else:
        out_all = lax.all_gather(out_weight, "shard", axis=0, tiled=True)
        out_own = lax.dynamic_index_in_dim(
            out_all.reshape(2, 2, part, width_d), core, 1, keepdims=False
        ).reshape(2 * part, width_d)
    if shards == 2:
        later = assemble(down_now, up_now, core[None].astype(jnp.int32))
    else:
        up_part = pick_columns(
            up_now, 2 * jnp.arange(shards, dtype=jnp.int32) + core, hidden_half
        )
        later = jnp.concatenate(
            [half_of(down_now, core)]
            + [up_part[:, k * width_d : (k + 1) * width_d] for k in range(2)],
            axis=0,
        )
    vectors_one, later = lax.optimization_barrier((vectors_one, later))
    later = lax.all_gather(later, "shard", axis=0)
    own_rows = later.shape[1] - 2 * rows_w
    down_own = later[:, :own_rows].reshape(-1, width_d)
    up_own = jnp.concatenate(
        [
            later[:, own_rows + k * rows_w : own_rows + (k + 1) * rows_w].reshape(-1, width_d)
            for k in range(2)
        ],
        axis=1,
    )

    block_base = (hi * QUAD + member) * tok_rows
    quad_base = hi * quad_rows
    own_seg = segments_at(starts, block_base + jnp.arange(tok_rows, dtype=jnp.int32))
    one_hot = (own_seg[:, None] == jnp.arange(slots, dtype=jnp.int32)[None, :]).astype(bf16)
    features_all = time_features(stamps_all.reshape(-1)).astype(bf16).reshape(shards, slots, TEMB)
    features_docs = time_features(doc_time[0]).astype(bf16)
    features = times(one_hot, features_docs).astype(bf16)
    quad_places = quad_base + jnp.arange(quad_rows, dtype=jnp.int32)
    quad_begin = begins_at(starts, quad_places)
    quad_end = ends_at(starts, quad_places, length)
    cosine, signed_sine = turn_tables(quad_places - quad_begin)
    reach = jnp.concatenate(
        [
            (quad_begin - quad_base)[None],
            (quad_end - quad_base)[None],
            jnp.zeros((6, quad_rows), jnp.int32),
        ],
        axis=0,
    )

    valid = valid_mask[0].astype(f32)
    counted = jnp.full((8, LANES), jnp.sum(valid))
    counted = sum_all(counted, "core", [1])
    counted = sum_all(sum_all(counted, "shard", bits_of("shard")), "lo", [1])

    block_in = tokens[0].astype(f32)
    _, normed_one, scales_one, inv_one = norm_forward(
        block_in, vectors_one[0], vectors_one[1], features, time_attn
    )
    quad_seg = segments_at(starts, quad_places)
    quad_hot = (quad_seg[:, None] == jnp.arange(slots, dtype=jnp.int32)[None, :]).astype(bf16)
    quad_features = times(quad_hot, features_docs).astype(bf16)
    projected = None
    for far in range(2):
        projected = project(
            jnp.stack([member ^ (2 * far), left_shard]).astype(jnp.int32),
            block_tokens[2 * far],
            block_tokens[2 * far + 1],
            quad_features,
            time_attn,
            vectors_one,
            qkv_left,
            qkv_right,
            cosine,
            signed_sine,
            projected,
        )
    act_quad, query_low, kv_pair = projected
    up_pairs = [(i, i + 1) for i in range(groups - 1)]
    down_pairs = [(i + 1, i) for i in range(groups - 1)]
    kv_prev = lax.ppermute(kv_pair, "hi", up_pairs)
    kv_next = lax.ppermute(kv_pair, "hi", down_pairs)

    query_low, counted = lax.optimization_barrier((query_low, counted))

    def ranges(row_shift, row_block, col_shift, col_block):
        return block_ranges(
            starts,
            length,
            quad_base + row_shift,
            row_block,
            quad_base + col_shift,
            col_block,
            quad_rows,
        )

    acc, stat = attend_near(
        ranges(0, BLOCK_Q, 0, BLOCK_K), query_low, kv_pair, reach
    )
    counted = sum_all(counted, "hi", [1])
    counted, acc = lax.optimization_barrier((counted, acc))
    counted = sum_all(counted, "hi", bits_of("hi")[1:])
    mixed_quad, lse = attend_far(
        ranges(0, BLOCK_Q, -quad_rows, BLOCK_K),
        ranges(0, BLOCK_Q, quad_rows, BLOCK_K),
        query_low,
        kv_prev,
        kv_next,
        reach,
        acc,
        stat,
    )

    def to_chip(value):
        kept, sent = half_of(value, lo), half_of(value, 1 - lo)
        return in_order(lo, kept, flip(sent, "lo"), 1)

    def to_quad(value):
        left, right = value[:, :part], value[:, part:]
        kept = jnp.where(lo == 0, left, right)
        sent = jnp.where(lo == 0, right, left)
        return in_order(lo, kept, flip(sent, "lo"), 0)

    def both_cores(value):
        return in_order(core, value, flip(value, "core"), 0)

    def summed_over_cores(far_part, own_part):
        return own_part + flip(far_part.astype(bf16), "core").astype(f32)

    def own_first(value):
        return jnp.concatenate([value, flip(value, "core")], axis=0)

    counted, mixed_quad = lax.optimization_barrier((counted, mixed_quad))
    counted = counted[0, 0]
    mixed_low = to_chip(mixed_quad)
    middle = block_in + summed_over_cores(
        times(half_of(mixed_low, 1 - core), out_own), times(half_of(mixed_low, core), out_own)
    )

    act_pre_two, normed_two, scales_two, inv_two = norm_forward(
        middle, gain_mlp, bias_mlp, features, time_mlp
    )
    act_two = own_first(act_pre_two.astype(bf16))
    upper_in = times(act_two, up_own) + up_bias_own.astype(f32)[None, :]
    normal_cdf = 0.5 + 0.5 * lax.erf(upper_in * math.sqrt(0.5))
    density = jnp.exp(-0.5 * upper_in * upper_in) * (1.0 / math.sqrt(2.0 * math.pi))
    hidden = (upper_in * normal_cdf).astype(bf16)
    slope = (normal_cdf + upper_in * density).astype(bf16)
    block_out = (
        middle
        + summed_over_cores(times(hidden[tok_rows:], down_own), times(hidden[:tok_rows], down_own))
        + down_bias_full.astype(f32)[None, :]
    )
    misfit = block_out - teacher[0].astype(f32)
    square_sum = jnp.sum(valid[:, None] * misfit * misfit)
    grad_final = (
        cotangent[0].astype(f32) + 2.0 / (counted * width_d) * valid[:, None] * misfit
    )
    grad_mid_own = grad_final.astype(bf16)
    grad_mid = own_first(grad_mid_own)
    grad_down_bias = jnp.sum(grad_mid_own.astype(f32), axis=0, keepdims=True)
    grad_upper = (times_trans(grad_mid, down_own) * slope.astype(f32)).astype(bf16)
    grad_up_bias = jnp.sum(grad_upper.astype(f32), axis=0)
    grad_act_two = summed_over_cores(
        times_trans(grad_upper[tok_rows:], up_own), times_trans(grad_upper[:tok_rows], up_own)
    )
    grad_in_two, grad_gain_two, grad_bias_two, by_doc_two = norm_backward(
        grad_act_two, normed_two, scales_two, inv_two, one_hot
    )
    grad_middle = grad_final + grad_in_two
    grad_branch = both_cores(grad_middle.astype(bf16))
    grad_mixed = times_trans(grad_branch, out_own).astype(bf16)
    grad_quad = to_quad(grad_mixed)
    late_upper, late_mid, _ = lax.optimization_barrier((grad_upper, grad_mid, grad_mixed))
    grad_down = contract_rows(hidden, late_mid)
    grad_up = contract_rows(act_two, late_upper)
    grad_out = contract_rows(mixed_low, grad_branch)

    if shards == 2:
        out_rows = grad_out
    else:
        by_core = lax.all_gather(grad_out.astype(bf16), "core", axis=0, tiled=False)
        out_rows = jnp.transpose(
            by_core.reshape(2, 2, part, width_d), (1, 0, 2, 3)
        ).reshape(2 * 2 * part, width_d)
    pairs = 2 * groups
    blocks = [
        grad_down.astype(bf16).reshape(shards, pairs, -1, width_d),
        jnp.concatenate(
            [
                grad_up[:, k * width_d : (k + 1) * width_d]
                .astype(bf16)
                .reshape(shards, pairs, -1, width_d)
                for k in range(2)
            ],
            axis=2,
        ),
        out_rows.astype(bf16).reshape(shards, pairs, -1, width_d),
    ]
    pieces = jnp.concatenate(blocks, axis=2).reshape(-1, width_d)
    pieces = lax.optimization_barrier((pieces, grad_quad))[0]
    reduced = lax.psum_scatter(pieces, ("shard", "lo"), scatter_dimension=0, tiled=True)
    head_of = jnp.arange(part, dtype=jnp.int32) // HEAD
    summing = (jnp.arange(8, dtype=jnp.int32)[:, None] == head_of[None, :]).astype(f32)
    delta = lax.dot_general(
        summing,
        grad_quad.astype(f32) * mixed_quad.astype(f32),
        (((1,), (1,)), ((), ())),
        precision=lax.Precision.HIGHEST,
        preferred_element_type=f32,
    )

    def give_back(row_shift, kv, dq):
        return attend_return(
            row_shift,
            ranges(row_shift, BLOCK_K, 0, BLOCK_Q),
            query_low,
            grad_quad,
            kv,
            reach,
            lse,
            delta,
            dq,
        )

    dq, dkv_prev = give_back(-quad_rows, kv_prev, None)
    from_next = lax.ppermute(dkv_prev, "hi", down_pairs)
    dq, dkv_next = give_back(quad_rows, kv_next, dq)
    from_prev = lax.ppermute(dkv_next, "hi", up_pairs)
    dq, dkv_own = give_back(0, kv_pair, dq)

    act_send, act_keep, qkv_send, qkv_keep = unproject(
        jnp.stack([lo, left_shard]).astype(jnp.int32),
        dq,
        dkv_own,
        from_next,
        from_prev,
        cosine,
        signed_sine,
        act_quad,
        qkv_own,
    )
    act_got = flip(act_send, "lo")
    if shards == 2:
        qkv_rows = qkv_keep + flip(qkv_send, "shard").astype(f32)
    else:
        qkv_rows = jnp.concatenate([qkv_keep, qkv_send.astype(f32)], axis=0)
        qkv_rows = scatter_sum(qkv_rows, "shard", reversed(bits_of("shard")))
    qkv_rows = scatter_sum(qkv_rows, "hi", bits_of("hi")[:1])
    act_got, qkv_rows = lax.optimization_barrier((act_got, qkv_rows))
    grad_chip = act_keep + act_got.astype(f32)
    grad_act_one = summed_over_cores(half_of(grad_chip, 1 - core), half_of(grad_chip, core))
    grad_in_one, grad_gain_one, grad_bias_one, by_doc_one = norm_backward(
        grad_act_one, normed_one, scales_one, inv_one, one_hot
    )
    input_grad = grad_middle + grad_in_one

    bias_slots = jnp.where(
        jnp.arange(2, dtype=jnp.int32)[None, :, None] == core,
        grad_up_bias.reshape(shards, 1, hidden_half),
        0.0,
    ).reshape(-1, width_d)
    square_top = square_sum.astype(bf16).astype(f32)
    loss_row = jnp.where(jnp.arange(width_d)[None, :] == 0, square_top, square_sum - square_top)
    summed_rows = [grad_gain_one, grad_bias_one, grad_gain_two, grad_bias_two, grad_down_bias]
    small = jnp.concatenate(
        summed_rows + [bias_slots, loss_row, by_doc_one, by_doc_two],
        axis=0,
    )
    filled = small.shape[0]
    small = jnp.pad(small, ((0, -filled % 16), (0, 0)))
    small = small.astype(bf16)
    qkv_rows = scatter_sum(qkv_rows, "hi", bits_of("hi")[1:]).astype(bf16)
    reduced = lax.optimization_barrier((reduced, dkv_own))[0]
    reduced = lax.psum_scatter(reduced, "hi", scatter_dimension=0, tiled=True)
    down_rows, up_rows, out_piece = (b.shape[2] for b in blocks)
    up_rows = up_rows // 2
    if shards == 2:
        part_rows = qkv_rows.shape[0] // QUAD
        turned = [
            jnp.concatenate(
                [
                    qkv_rows[k * part_rows : (k + 1) * part_rows, t * part : (t + 1) * part]
                    for k in range(QUAD)
                ],
                axis=1,
            )
            for t in range(3)
        ]
        reduced = lax.optimization_barrier((reduced, act_got))[0]
        everyone = lax.all_gather(reduced, ("hi", "lo", "core"), axis=0)
        everyone = everyone.reshape(QUAD * groups, -1, width_d)
        rest = jnp.concatenate(turned + [small], axis=0)
        rest = gather_back(gather_back(rest, "hi"), "lo")
        everyone, rest = lax.optimization_barrier((everyone, rest))
        rest = gather_back(rest, "core")
        rest = rest.reshape(QUAD * groups, -1, width_d)
        small = rest[:, rest.shape[1] - small.shape[0] :]
        down_total, up_total, out_total = lay_out(
            everyone, groups, hidden_half, down_rows, up_rows, out_piece
        )
        places = jnp.stack([2 * core + lo, bit_mirror(hi, groups)]).astype(jnp.int32)
        qkv_total = unfold(rest, places, groups, qkv_rows.shape[0])
    else:
        everyone = lax.all_gather(
            jnp.concatenate([reduced, small], axis=0), ("hi", "lo", "core"), axis=0
        ).reshape(QUAD * groups, -1, width_d)
        filled = everyone.shape[1] - small.shape[0]
        small = everyone[:, filled:]
        everyone = everyone[:, :filled].reshape(pairs, 2, -1, width_d)
        wide = everyone.astype(f32).reshape(groups, 2, 2, -1, width_d)
        wide = jnp.transpose(wide, (1, 0, 2, 3, 4)).reshape(everyone.shape)
        down_total = jnp.transpose(wide[:, :, :down_rows], (1, 0, 2, 3)).reshape(-1, width_d)
        up_piece = wide[:, :, down_rows : down_rows + 2 * up_rows]
        up_piece = up_piece.reshape(pairs, 2, 2, up_rows, shards // 2, hidden_half)
        up_total = jnp.transpose(up_piece, (0, 3, 2, 4, 1, 5)).reshape(rows_w, 4 * width_d)
        out_total = wide[:, 0, down_rows + 2 * up_rows :].reshape(-1, width_d)
        for axis in ("hi", "lo", "core"):
            qkv_rows = gather_back(qkv_rows, axis)
        qkv_total = spread(
            qkv_rows.reshape(QUAD * groups, rows_w // groups, 3 * part),
            jnp.stack([2 * core + lo, bit_mirror(hi, groups)]).astype(jnp.int32),
            groups,
        )

    small = jnp.sum(small.astype(f32), axis=0)
    small_all = gather_shard(small).reshape(shards, -1, width_d)
    bias_rows = bias_slots.shape[0]
    head_rows = 6 + bias_rows
    totals = jnp.sum(small_all[:, :head_rows], axis=0)
    docs_one = small_all[:, head_rows : head_rows + slots]
    docs_two = small_all[:, head_rows + slots : head_rows + 2 * slots]

    def own_vector(row):
        return lax.dynamic_slice_in_dim(row, shard * own_part, own_part, 0)

    own_features = lax.dynamic_slice_in_dim(
        features_all, shard * (TEMB // shards), TEMB // shards, 2
    ).astype(f32)

    def time_total(docs):
        return lax.dot_general(
            own_features,
            docs,
            (((0, 1), (0, 1)), ((), ())),
            precision=lax.Precision.HIGHEST,
            preferred_element_type=f32,
        )

    up_bias_total = lax.dynamic_slice_in_dim(
        totals[5 : 5 + bias_rows].reshape(-1), shard * 2 * hidden_half, 2 * hidden_half, 0
    )
    loss_row = totals[5 + bias_rows]
    loss_value = (loss_row[0] + loss_row[1]) / (counted * width_d)
    return (
        block_out.astype(bf16)[None],
        loss_value,
        input_grad[None],
        own_vector(totals[0]),
        own_vector(totals[1]),
        time_total(docs_one),
        qkv_total,
        out_total,
        own_vector(totals[2]),
        own_vector(totals[3]),
        time_total(docs_two),
        up_total,
        up_bias_total,
        down_total,
        own_vector(totals[4]),
    )


def solution(mesh):
    ctx, shards = mesh.shape["ctx"], mesh.shape["shard"]
    fine = Mesh(
        mesh.devices.reshape(ctx // QUAD, 2, 2, shards), ("hi", "lo", "core", "shard")
    )
    blocks = ("hi", "lo", "core")
    in_specs = (
        P("shard", blocks, None),
        P("shard", blocks, None),
        P("shard", blocks, None),
        P("shard", None),
        P("shard", None),
        P("shard", blocks),
        P("shard"),
        P("shard"),
        P("shard", None),
        P("shard", None),
        P("shard", None),
        P("shard"),
        P("shard"),
        P("shard", None),
        P("shard", None),
        P("shard"),
        P("shard", None),
        P("shard"),
    )
    out_specs = (
        P("shard", blocks, None),
        P(),
        P("shard", blocks, None),
        P("shard"),
        P("shard"),
        P("shard", None),
        P("shard", None),
        P("shard", None),
        P("shard"),
        P("shard"),
        P("shard", None),
        P("shard", None),
        P("shard"),
        P("shard", None),
        P("shard"),
    )
    return jax.shard_map(
        on_device, mesh=fine, in_specs=in_specs, out_specs=out_specs, check_vma=False
    )
```
